512 devices in a mesh: orb: 16 (over z), space: 32 (over y, x, core).
Axes of the slice: x: 4, y: 4, z: 16, core: 2. Of those that a mesh axis runs over, the one named last changes fastest.
Arguments:
- orbitals: float32 [32, 512, 128], P('orb', 'space'), may hold values from 0 to 0.25
- points: float32 [3, 512, 128], P(None, 'space')
- quad_weight: float32 [512, 128], P('space'), may hold values from 0.5 to 2
- external: float32 [512, 128], P('space'), may hold values from -3 to 1
- screening: float32 [32], replicated, may hold values from 0.05 to 2
- level_index: int32 [32], P('orb'), may hold values from 0 to 31
- near_cells: int32 [512, 27], P('space'), may hold values from -1 to 511, as said below
- far_cells: int32 [512, 42], P('space'), may hold values from -1 to 511, as said below
Outputs:
- new_orbitals: float32 [32, 512, 128], P('orb', 'space')
- hartree: float32 [512, 128], P('space')
The draws below stay inside these ranges and needn't reach their ends.
Inputs may be any that keep to these rules, and one draw needn't show every extreme that they name: `near_cells`: row t lists distinct cells in increasing order, then -1: every cell of its own plane whose first two box indices differ from those of t by at most one (t itself among them), the cells directly above and below t, and some of the other cells of the two adjacent planes whose first two box indices differ from those of t by at most one. Some row holds 27 cells. `far_cells`: row t lists in increasing order, then -1, all cells of the planes floor(t / 16) - 1 to floor(t / 16) + 1 that are not in row t of near_cells. Some row holds 42 cells.
All inputs are finite; a program needn't handle non-finite values.
Results may differ from the reference program's by a relative error of at most 0.0003.
Values sent between devices are 32-bit elements; how exact they have to be, the bound alone decides.
A program may use at most 64 MiB of HBM per device.

```python
import math
import jax
import jax.numpy as jnp
from jax import lax

ORBS = 32
PTS = 128
NODES = 4
NKAPPA = 32
NNEAR = 27
NFAR = 42
CELLS = 512


def draw_points(key, part):
    scaled = jax.random.uniform(jax.random.fold_in(key, 4409), (3, CELLS, PTS), jnp.float32)
    cell_ids = jnp.arange(CELLS, dtype=jnp.int32)
    corners = jnp.stack([cell_ids % 4, cell_ids // 4 % 4, cell_ids // 16]).astype(jnp.float32)
    return (corners[:, :, None] + scaled) * 0.25


def neighbour_lists(key):
    keys = jax.random.split(jax.random.fold_in(key, 7301), 5)
    planes = CELLS // 16
    choices_bits = jax.random.randint(keys[0], (CELLS, 48), 0, 2)
    pick_inner = jax.random.randint(keys[1], (), 0, 4)
    plane_inner = jax.random.randint(keys[2], (), 1, planes - 1)
    pick_corner = jax.random.randint(keys[3], (), 0, 4)
    plane_corner = jax.random.randint(keys[4], (), 1, planes - 1)
    full_cell = 16 * plane_inner + 5 + pick_inner % 2 + 4 * (pick_inner // 2)
    empty_cell = 16 * plane_corner + 3 * (pick_corner % 2) + 12 * (pick_corner // 2)
    target = jnp.arange(CELLS, dtype=jnp.int32)[:, None]
    slot = jnp.arange(48, dtype=jnp.int32)[None, :]
    level = target // 16 + slot // 16 - 1
    within = slot % 16
    candidate = level * 16 + within
    valid = (level >= 0) & (level < planes)
    close_x = jnp.abs(within % 4 - target % 4) <= 1
    close_y = jnp.abs(within // 4 - target // 4 % 4) <= 1
    flat_plane = slot // 16 == 1
    face_cell = within == target % 16
    bits_now = jnp.where(target == full_cell, 1, jnp.where(target == empty_cell, 0, choices_bits))
    near_flag = valid & close_x & close_y & (flat_plane | face_cell | (bits_now == 1))
    far_flag = valid & jnp.logical_not(near_flag)
    near_order = jnp.argsort(jnp.where(near_flag, 0, 1), axis=1, stable=True)
    far_order = jnp.argsort(jnp.where(far_flag, 0, 1), axis=1, stable=True)
    near_list = jnp.take_along_axis(jnp.where(near_flag, candidate, -1), near_order, axis=1)[:, :NNEAR]
    far_list = jnp.take_along_axis(jnp.where(far_flag, candidate, -1), far_order, axis=1)[:, :NFAR]
    return (near_list.astype(jnp.int32), far_list.astype(jnp.int32))


def draw_near_cells(key, part):
    return neighbour_lists(key)[0]


def draw_far_cells(key, part):
    return neighbour_lists(key)[1]


def plant(result, stream_key, least, top_value):
    shape = result.shape
    index_at = [jax.random.randint(jax.random.fold_in(stream_key, axis), (), 0, shape[axis]) for axis in range(len(shape))]
    result = result.at[tuple(index_at)].set(least)
    longest = shape.index(max(shape))
    index_at[longest] = (index_at[longest] + 1) % shape[longest]
    return result.at[tuple(index_at)].set(top_value)


def shard_levels(rng, shape, pieces, smallest, high):
    gain, own = 1.0, jax.random.fold_in(rng, 6)
    for position, parts in pieces:
        steps = jnp.exp(jax.random.uniform(jax.random.fold_in(own, position), (parts,), jnp.float32, smallest / len(pieces), high / len(pieces)))
        gain = gain * jnp.repeat(steps, shape[position] // parts).reshape([-1 if axis == position else 1 for axis in range(len(shape))])
    return gain


def setup_inputs(seed: int = 0) -> dict:
    splits = jax.random.split(jax.random.key(seed), 9)
    orbitals = jnp.clip(0.25 * jax.random.uniform(splits[0], (ORBS, CELLS, PTS), jnp.float32) ** shard_levels(splits[0], (ORBS, CELLS, PTS), ((0, 16), (1, 32)), -0.2, 0.2), 0.0, 0.25)
    points = draw_points(jax.random.fold_in(splits[8], 71), 0)
    quad_weight = jnp.clip(jnp.exp(math.log(2.0) - 1.3862944 * jax.random.uniform(splits[2], (CELLS, PTS), jnp.float32) ** shard_levels(splits[2], (CELLS, PTS), ((0, 32),), -0.2, 0.2)), 0.5, 2.0)
    external = jnp.clip(-3.0 + 4.0 * jax.random.uniform(splits[3], (CELLS, PTS), jnp.float32) ** shard_levels(splits[3], (CELLS, PTS), ((0, 32),), -0.2, 0.2), -3.0, 1.0)
    screening = jnp.clip(jnp.exp(jax.random.uniform(splits[4], (NKAPPA,), jnp.float32, math.log(0.05), math.log(2.0))), 0.05, 2.0)
    level_index = plant(jax.random.randint(splits[5], (ORBS,), 0, NKAPPA), jax.random.fold_in(splits[5], 1), 0, NKAPPA - 1).astype(jnp.int32)
    near_cells = draw_near_cells(jax.random.fold_in(splits[8], 71), 0)
    far_cells = draw_far_cells(jax.random.fold_in(splits[8], 71), 0)
    return dict(orbitals=orbitals, points=points, quad_weight=quad_weight, external=external, screening=screening, level_index=level_index, near_cells=near_cells, far_cells=far_cells)


cell_side = 0.25
soften = 6.25e-06
green_scale = -0.5 / math.pi

def cheb_nodes(node_count):
    indices = jnp.arange(node_count, dtype=jnp.int32).astype(jnp.float32)
    return jnp.cos((2.0 * indices + 1.0) * (math.pi / (2.0 * node_count)))

def lagrange(scaled, node_set, node_count):
    factors = []
    for outer_node in range(node_count):
        running = jnp.ones_like(scaled)
        for inner_node in range(node_count):
            if inner_node != outer_node:
                running = running * ((scaled - node_set[inner_node]) / (node_set[outer_node] - node_set[inner_node]))
        factors.append(running)
    return jnp.stack(factors)

def anterp(locations, corners, extent):
    node_set = cheb_nodes(NODES)
    scaled = 2.0 * (locations - corners[:, :, None]) / extent[:, None, None] - 1.0
    basis_x = lagrange(scaled[0], node_set, NODES)
    basis_y = lagrange(scaled[1], node_set, NODES)
    basis_z = lagrange(scaled[2], node_set, NODES)
    weights = basis_x[:, None, None] * basis_y[None, :, None] * basis_z[None, None, :]
    return weights.reshape((NODES * NODES * NODES,) + locations.shape[1:])

def proxies(corners, extent):
    node_set = cheb_nodes(NODES)
    offset = 0.5 * (node_set + 1.0)
    grid_shape = (NODES, NODES, NODES) + corners.shape[1:]
    grid_x = jnp.broadcast_to((corners[0][None, :] + offset[:, None] * extent[0])[:, None, None], grid_shape)
    grid_y = jnp.broadcast_to((corners[1][None, :] + offset[:, None] * extent[1])[None, :, None], grid_shape)
    grid_z = jnp.broadcast_to((corners[2][None, :] + offset[:, None] * extent[2])[None, None, :], grid_shape)
    stacked = jnp.stack([grid_x, grid_y, grid_z]).reshape((3, NODES * NODES * NODES) + corners.shape[1:])
    return jnp.moveaxis(stacked, 1, 2)

def cell_lows(cell_ids):
    return jnp.stack([cell_ids % 4, cell_ids // 4 % 4, cell_ids // 16]).astype(jnp.float32) * cell_side

def plane_lows(levels):
    zeroes = jnp.zeros_like(levels)
    return jnp.stack([zeroes, zeroes, levels]).astype(jnp.float32) * cell_side

def cell_extent():
    return jnp.full((3,), cell_side, jnp.float32)

def plane_extent():
    return jnp.array([4.0 * cell_side, 4.0 * cell_side, cell_side], jnp.float32)

def kernel_sum(targets, locations, values, decay_rates):
    squared = jnp.zeros((targets.shape[1], locations.shape[1]), jnp.float32)
    for component in range(3):
        difference = targets[component][:, None] - locations[component][None, :]
        squared = squared + difference * difference
    distance = jnp.sqrt(squared + soften)
    kernel = jnp.exp(-decay_rates[:, None, None] * distance[None]) / distance[None]
    return lax.optimization_barrier(jnp.sum(kernel * values[:, None, :], axis=2))

def cell_moments(mapping, values):
    return jnp.einsum('pcj,rcj->rcp', mapping, values, precision=lax.Precision.HIGHEST)

def plane_moments(mapping, values):
    grouped = values.reshape(values.shape[0], mapping.shape[1], -1)
    return jnp.einsum('pgj,rgj->rgp', mapping, grouped, precision=lax.Precision.HIGHEST)

def evaluate(points, values, cell_mom, plane_proxy, plane_mom, near_cells, far_cells, decay_rates):
    kinds = values.shape[0]
    levels = jnp.arange(plane_mom.shape[1], dtype=jnp.int32)
    extent = cell_extent()

    def per_cell(target):
        near_ids = near_cells[target]
        near_live = (near_ids >= 0).astype(jnp.float32)
        near_slot = jnp.maximum(near_ids, 0)
        near_src = points[:, near_slot, :].reshape(3, -1)
        near_val = (values[:, near_slot, :] * near_live[None, :, None]).reshape(kinds, -1)
        far_ids = far_cells[target]
        far_live = (far_ids >= 0).astype(jnp.float32)
        far_slot = jnp.maximum(far_ids, 0)
        far_src = proxies(cell_lows(far_slot), extent).reshape(3, -1)
        far_val = (cell_mom[:, far_slot, :] * far_live[None, :, None]).reshape(kinds, -1)
        plane_keep = (jnp.abs(levels - target // 16) >= 2).astype(jnp.float32)
        coarse_val = (plane_mom * plane_keep[None, :, None]).reshape(kinds, -1)
        points_here = points[:, target, :]
        return kernel_sum(points_here, near_src, near_val, decay_rates) + kernel_sum(points_here, far_src, far_val, decay_rates) + kernel_sum(points_here, plane_proxy, coarse_val, decay_rates)
    return lax.map(per_cell, jnp.arange(points.shape[1], dtype=jnp.int32))

def reference(orbitals, points, quad_weight, external, screening, level_index, near_cells, far_cells):
    cell_count = points.shape[1]
    planes = cell_count // 16
    weight = quad_weight * (cell_side ** 3 / PTS)
    density = 2.0 * lax.optimization_barrier(jnp.sum(orbitals * orbitals, axis=0))
    cell_map = anterp(points, cell_lows(jnp.arange(cell_count, dtype=jnp.int32)), cell_extent())
    levels = jnp.arange(planes, dtype=jnp.int32)
    plane_map = anterp(points.reshape(3, planes, -1), plane_lows(levels), plane_extent())
    plane_proxy = proxies(plane_lows(levels), plane_extent()).reshape(3, -1)
    charge = (weight * density)[None]
    charge_mom = cell_moments(cell_map, charge)
    charge_plane = plane_moments(plane_map, charge)
    hartree = evaluate(points, charge, charge_mom, plane_proxy, charge_plane, near_cells, far_cells, jnp.zeros((1,), jnp.float32))[:, 0, :]
    potential = external + hartree
    sources = (weight * potential)[None] * orbitals
    source_mom = cell_moments(cell_map, sources)
    source_plane = plane_moments(plane_map, sources)
    decay_rates = screening[level_index]
    updated = green_scale * evaluate(points, sources, source_mom, plane_proxy, source_plane, near_cells, far_cells, decay_rates)
    return (jnp.transpose(updated, (1, 0, 2)), hartree)
```

```python
import functools
import math

import jax
import jax.numpy as jnp
from jax import lax
from jax.experimental import pallas as pl
from jax.experimental.pallas import tpu as pltpu
from jax.sharding import PartitionSpec as P

F32 = jnp.float32
BF16 = jnp.bfloat16
HI = lax.Precision.HIGHEST
LANES = (((1,), (1,)), ((), ()))
SOFTEN = 6.25e-06
SCALE = -0.5 / math.pi
SIDE = 0.25
NODE = [math.cos((2 * a + 1) * math.pi / 8) for a in range(4)]
OFFSET = [0.5 * (t + 1.0) for t in NODE]
FAR = 12
PLANE = 8
DENSE = FAR + PLANE
NEAR = 4 * 6 + 8 * 9 + 4 * 14


def iota(shape, axis):
    return lax.broadcasted_iota(jnp.int32, shape, axis)


def pick(index, table):
    out = jnp.full(index.shape, table[0], F32)
    for i in range(1, 4):
        out = jnp.where(index == i, F32(table[i]), out)
    return out


def pick_scalar(index, table):
    out = F32(table[0])
    for i in range(1, 4):
        out = jnp.where(index == i, F32(table[i]), out)
    return out


def select_rows(row, parts):
    out = jnp.where(row == 0, parts[0], parts[1])
    for i in range(2, 4):
        out = jnp.where(row == i, parts[i], out)
    return out


def lagrange(u):
    out = []
    for a in range(4):
        term = None
        for n in range(4):
            if n != a:
                factor = (u - NODE[n]) * (1.0 / (NODE[a] - NODE[n]))
                term = factor if term is None else term * factor
        out.append(term)
    return out


def near_count(t):
    cx, cy = t % 4, t // 4
    nx = jnp.where((cx == 0) | (cx == 3), 2, 3)
    ny = jnp.where((cy == 0) | (cy == 3), 2, 3)
    return 3 * nx * ny


def hi_lo(row):
    r = iota((16, row.shape[1]), 0)
    rest = row - row.astype(BF16).astype(F32)
    return jnp.where(r == 0, row, jnp.where(r == 1, rest, 0.0)).astype(BF16)


def kernel(
    orb, pts, qw, ext, screening, level, near, out, hart,
    G, TB, DXY, PR, CV, SV, MC, MS, LG, LP, A, AP, D0, D1, RA, RB,
    ZCO, ZCR, ZSO, ZSR, ZF, HG, FM, VN, VF, VP, send, recv,
):
    o = lax.axis_index("orb")
    g = lax.axis_index("space")
    core, x, y = g % 2, g // 2 % 4, g // 8
    zi, zb = o % 4, o // 4
    up, down = (g + 1) % 32, (g + 31) % 32
    lane = iota((1, 128), 1)

    def other_z(d):
        return {"orb": (o + d) % 16}

    def other_x(d):
        return {"space": g + 2 * ((x + d) % 4 - x)}

    def other_y(d):
        return {"space": g + 8 * ((y + d) % 4 - y)}

    barrier = pltpu.get_barrier_semaphore()
    partners = [other_z(d) for d in range(1, 16)]
    partners += [other_x(d) for d in range(1, 4)] + [other_y(d) for d in range(1, 4)]
    partners += [{"space": up}, {"space": down}]
    for partner in partners:
        pl.semaphore_signal(barrier, inc=1, device_id=partner, device_id_type=pl.DeviceIdType.MESH)

    def copy(src, dst, i, device, j=None):
        return pltpu.make_async_remote_copy(
            src, dst, send.at[i], recv.at[i if j is None else j],
            device_id=device, device_id_type=pl.DeviceIdType.MESH,
        )

    def rim(ref, i):
        return [
            copy(ref.at[1], ref.at[0], i, {"space": up}),
            copy(ref.at[1], ref.at[2], i + 1, {"space": down}),
        ]

    def begin(copies):
        for c in copies:
            c.start()

    def finish(copies):
        for c in copies:
            c.wait()

    rates = [-screening[level[v]] * (1.0 / math.log(2.0)) for v in range(2)]

    def columns(t):
        for k in range(3):
            TB[k] = jnp.broadcast_to(pts[k, pl.ds(t, 1), :], (128, 128)).T

    def green(r2):
        inv = lax.rsqrt(r2)
        s = r2 * inv
        return [(jnp.exp2(s * rate) * inv).astype(BF16) for rate in rates]

    def far_xy():
        a, b, c8 = lane // 4 % 4, lane % 4, lane // 16
        gx = (c8 % 4).astype(F32) * SIDE + SIDE * pick(a, OFFSET)
        dx = TB[0] - gx
        for half in range(2):
            gy = (c8 // 4 + 2 * half).astype(F32) * SIDE + SIDE * pick(b, OFFSET)
            dy = TB[1] - gy
            DXY[half] = dx * dx + (dy * dy + SOFTEN)

    def plane_z():
        gz = (lane // 4).astype(F32) * SIDE + SIDE * pick(lane % 4, OFFSET)
        dz = TB[2] - gz
        DXY[0] = dz * dz + SOFTEN

    def far_dz2(k):
        dz = TB[2] - ((g - 1 + k // 4).astype(F32) * SIDE + SIDE * pick_scalar(k % 4, OFFSET))
        return dz * dz

    def plane_xy2(ab):
        dx = TB[0] - pick_scalar(ab // 4, OFFSET)
        dy = TB[1] - pick_scalar(ab % 4, OFFSET)
        return dx * dx + dy * dy

    def store_green(block, half, r2):
        for v, values in enumerate(green(r2)):
            G[block, v, :, half * 128 : half * 128 + 128] = values

    def dense(lo, hi):
        def cell(t, carry):
            columns(t)
            far_xy()

            def far(k, c):
                dz2 = far_dz2(k)
                for half in range(2):
                    store_green(t * DENSE + k, half, DXY[half] + dz2)
                return c

            lax.fori_loop(0, FAR, far, 0)
            plane_z()

            def planes(k, c):
                for half in range(2):
                    store_green(t * DENSE + FAR + k, half, plane_xy2(2 * k + half) + DXY[0])
                return c

            lax.fori_loop(0, PLANE, planes, 0)
            return carry

        lax.fori_loop(lo, hi, cell, 0)

    def near_slot(t, n):
        cell = near[t, jnp.minimum(n, 26)]
        slot = jnp.clip(cell - 16 * (g - 1), 0, 47)
        return jnp.where((cell >= 0) & (n < 27), slot, 48)

    def near_r2(slot):
        lev, c = slot // 16, slot % 16
        total = None
        for k in range(3):
            d = TB[k] - PR[lev, k, pl.ds(c, 1), :]
            total = d * d + SOFTEN if total is None else total + d * d
        return total

    def near_green(lo, hi, off):
        def cell(t, off):
            columns(t)
            count = (near_count(t) + 1) // 2

            def pair(p, c):
                for half in range(2):
                    store_green(
                        DENSE * 16 + off + p, half, near_r2(near_slot(t, 2 * p + half))
                    )
                return c

            lax.fori_loop(0, count, pair, 0)
            return off + count

        return lax.fori_loop(lo, hi, cell, off)

    D0[...] = 2.0 * (orb[0] * orb[0] + orb[1] * orb[1])
    PR[1] = pts[...]
    PR[3] = jnp.zeros((3, 16, 128), F32)
    CV[3] = jnp.zeros((16, 128), F32)
    row16 = iota((16, 128), 0)
    ux = (pts[0] - (row16 % 4).astype(F32) * SIDE) * (2.0 / SIDE) - 1.0
    uy = (pts[1] - (row16 // 4).astype(F32) * SIDE) * (2.0 / SIDE) - 1.0
    uz = (pts[2] - g.astype(F32) * SIDE) * (2.0 / SIDE) - 1.0
    for k, u in enumerate((ux, uy, uz)):
        for a, w in enumerate(lagrange(u)):
            LG[k, a] = w
    for k in range(2):
        for a, w in enumerate(lagrange(2.0 * pts[k] - 1.0)):
            LP[k, a] = w
    row8 = iota((8, 128), 0)
    for c in range(16):
        one = slice(c, c + 1)
        ycell = select_rows(row8 % 4, [LG[1, b, one, :] for b in range(4)])
        yplane = select_rows(row8 % 4, [LP[1, b, one, :] for b in range(4)])
        for k in range(2):
            xcell = jnp.where(row8 < 4, LG[0, 2 * k, one, :], LG[0, 2 * k + 1, one, :])
            xplane = jnp.where(row8 < 4, LP[0, 2 * k, one, :], LP[0, 2 * k + 1, one, :])
            at = c % 8 * 16 + k * 8
            A[c // 8, at : at + 8, :] = xcell * ycell
            AP[k * 8 : k * 8 + 8, c * 128 : c * 128 + 128] = xplane * yplane

    def masks(t, carry):
        lev = g - 1 + row8 // 2
        cell = lev * 16 + row8 % 2 * 8 + lane // 16
        hit = (lev < 0) | (lev > 31)
        for n in range(27):
            hit = hit | (cell == near[t, n])
        FM[t] = jnp.where(hit, 0.0, 1.0)
        return carry

    lax.fori_loop(0, 16, masks, 0)
    dense(0, 4)
    pl.semaphore_wait(barrier, len(partners))

    first = [copy(D0, RA.at[d - 1], d - 1, {"orb": zb * 4 + (zi + d) % 4}) for d in range(1, 4)]
    begin(first)
    edge_points = rim(PR, 6)
    begin(edge_points)
    dense(4, 7)
    finish(first)
    D1[...] = D0[...] + (RA[0] + RA[1]) + RA[2]
    second = [
        copy(D1, RB.at[d - 1], 2 + d, {"orb": (zb + d) % 4 * 4 + zi}) for d in range(1, 4)
    ]
    begin(second)
    dense(7, 12)
    finish(second)
    weight = qw[...] * (SIDE**3 / 128)
    CV[1] = weight * (D1[...] + (RB[0] + RB[1]) + RB[2])

    def moments(values, cells):
        tiles = []
        for c in range(16):
            one = slice(c, c + 1)
            z = select_rows(row8 % 4, [LG[2, d, one, :] for d in range(4)])
            parts = [v[one, :] for v in values]
            tiles.append(z * jnp.where(row8 < 4, parts[0], parts[1] if len(parts) > 1 else 0.0))
        for half in range(2):
            rows = jnp.concatenate(tiles[half * 8 : half * 8 + 8], axis=0)
            every = lax.dot_general(rows, A[half], LANES, precision=HI, preferred_element_type=F32)
            total = jnp.zeros((8, 128), F32)
            for c in range(8):
                total = jnp.where(lane // 16 == c, every[c * 8 : c * 8 + 8], total)
            cells[1, half] = total
        wide = jnp.concatenate(tiles, axis=1)
        small = lax.dot_general(AP[...], wide, LANES, precision=HI, preferred_element_type=F32)
        planes = []
        for v in range(len(values)):
            spread = (iota((8, 128), 0) == v * 4 + lane % 4).astype(F32)
            planes.append(jnp.dot(small, spread, precision=HI, preferred_element_type=F32))
        return planes

    def gather_planes(planes, own, got, base, fill):
        for v, plane in enumerate(planes):
            own[0, v] = plane
        stage = [copy(own.at[0], got.at[0], base, {"space": g + 1 - 2 * core})]
        begin(stage)
        fill[0]()
        finish(stage)
        own[1] = jnp.where(lane // 4 % 2 == core, own[0], got[0])
        stage = [copy(own.at[1], got.at[d], base + d, other_x(d)) for d in range(1, 4)]
        begin(stage)
        fill[1]()
        finish(stage)
        full = own[1]
        for d in range(1, 4):
            full = jnp.where(lane // 8 % 4 == (x + 4 - d) % 4, got[d], full)
        own[2] = full
        stage = [copy(own.at[2], got.at[3 + d], base + 3 + d, other_y(d)) for d in range(1, 4)]
        begin(stage)
        fill[2]()
        finish(stage)
        full = own[2]
        for d in range(1, 4):
            full = jnp.where(lane // 32 == (y + 4 - d) % 4, got[3 + d], full)
        return jnp.where(jnp.abs(lane // 4 - g) >= 2, full, 0.0)

    nothing = lambda: None
    edge_charge = rim(CV, 8)
    begin(edge_charge)
    planes = moments([CV.at[1]], MC)
    edge_moments = rim(MC, 10)
    begin(edge_moments)
    full = gather_planes(
        planes, ZCO, ZCR, 12, [nothing, lambda: dense(12, 14), lambda: dense(14, 16)]
    )
    ZF[...] = full[0]
    finish(edge_points)
    finish(edge_charge)
    finish(edge_moments)

    columns(o)
    acc = jnp.zeros((128, 128), F32)

    def near_hartree(p, acc):
        for half in range(2):
            slot = near_slot(o, 2 * p + half)
            acc = acc + lax.rsqrt(near_r2(slot)) * CV[slot // 16, pl.ds(slot % 16, 1), :]
        return acc

    acc = lax.fori_loop(0, (near_count(o) + 1) // 2, near_hartree, acc)
    far_xy()

    def far_hartree(k, acc):
        dz2 = far_dz2(k)
        for half in range(2):
            row = MC[k // 4, half, pl.ds(k % 4, 1), :] * FM[o, pl.ds(k // 4 * 2 + half, 1), :]
            acc = acc + lax.rsqrt(DXY[half] + dz2) * row
        return acc

    acc = lax.fori_loop(0, FAR, far_hartree, acc)
    plane_z()

    def plane_hartree(k, acc):
        for half in range(2):
            ab = 2 * k + half
            acc = acc + lax.rsqrt(plane_xy2(ab) + DXY[0]) * ZF[pl.ds(ab, 1), :]
        return acc

    acc = lax.fori_loop(0, PLANE, plane_hartree, acc)
    summed = lax.dot_general(
        jnp.ones((8, 128), F32), acc, LANES, precision=HI, preferred_element_type=F32
    )
    HG[o] = summed[0:1]
    shares = [copy(HG.at[o], HG.at[o], 18 + d, other_z(d), 19 + o) for d in range(1, 16)]
    begin(shares)
    off = near_green(0, 8, 0)
    for d in range(1, 16):
        shares[d - 1].wait_send()
        k = (o + 16 - d) % 16
        copy(HG.at[k], HG.at[k], 18 + d, other_z(d), 19 + k).wait_recv()
    for c in range(16):
        hart[c : c + 1, :] = HG[c]

    scaled = weight * (ext[...] + hart[...])
    for v in range(2):
        SV[1, v] = scaled * orb[v]
    edge_sources = rim(SV, 35)
    begin(edge_sources)
    planes = moments([SV.at[1, 0], SV.at[1, 1]], MS)
    edge_moments = rim(MS, 37)
    begin(edge_moments)
    cells = [off]

    def more(lo, hi):
        cells[0] = near_green(lo, hi, cells[0])

    full = gather_planes(
        planes, ZSO, ZSR, 39, [lambda: more(8, 10), lambda: more(10, 12), lambda: more(12, 16)]
    )
    finish(edge_sources)
    finish(edge_moments)

    for v in range(2):
        VN[v, 48] = jnp.zeros((16, 128), BF16)
        for lev in range(3):
            for c in range(16):
                VN[v, lev * 16 + c] = hi_lo(SV[lev, v, c : c + 1, :])
            for d in range(4):
                for half in range(2):
                    r = v * 4 + d
                    VF[lev * 4 + d, v, :, half * 128 : half * 128 + 128] = hi_lo(
                        MS[lev, half, r : r + 1, :]
                    )
        for ab in range(16):
            half = ab % 2
            VP[ab // 2, v, :, half * 128 : half * 128 + 128] = hi_lo(full[v, ab : ab + 1, :])

    def product(rows, block, v):
        return lax.dot_general(rows, G[block, v], LANES, preferred_element_type=F32)

    def update(t, off):
        acc = [jnp.zeros((16, 128), F32) for _ in range(2)]
        for lev in range(3):
            mask = jnp.concatenate(
                [
                    jnp.broadcast_to(FM[t, lev * 2 + half : lev * 2 + half + 1, :], (16, 128))
                    for half in range(2)
                ],
                axis=1,
            ).astype(BF16)
            for d in range(4):
                k = lev * 4 + d
                for v in range(2):
                    acc[v] = acc[v] + product(VF[k, v] * mask, t * DENSE + k, v)
        for k in range(PLANE):
            for v in range(2):
                acc[v] = acc[v] + product(VP[k, v], t * DENSE + FAR + k, v)
        count = (near_count(t) + 1) // 2

        def pair(p, acc):
            s0, s1 = near_slot(t, 2 * p), near_slot(t, 2 * p + 1)
            return tuple(
                acc[v]
                + product(
                    jnp.concatenate([VN[v, s0], VN[v, s1]], axis=1), DENSE * 16 + off + p, v
                )
                for v in range(2)
            )

        acc = lax.fori_loop(0, count, pair, tuple(acc))
        for v in range(2):
            out[v, pl.ds(t, 1), :] = SCALE * (acc[v][0:1] + acc[v][1:2])
        return off + count

    lax.fori_loop(0, 16, update, 0)


def body(orbitals, points, quad_weight, external, screening, level_index, near_cells, far_cells):
    vmem = pl.BlockSpec(memory_space=pltpu.VMEM)
    smem = pl.BlockSpec(memory_space=pltpu.SMEM)

    def f32(*shape):
        return pltpu.VMEM(shape, F32)

    def bf16(*shape):
        return pltpu.VMEM(shape, BF16)

    return pl.pallas_call(
        kernel,
        out_shape=(
            jax.ShapeDtypeStruct((2, 16, 128), F32),
            jax.ShapeDtypeStruct((16, 128), F32),
        ),
        in_specs=[vmem] * 4 + [smem] * 3,
        out_specs=(vmem, vmem),
        scratch_shapes=[
            bf16(16 * DENSE + NEAR, 2, 128, 256),
            f32(3, 128, 128),
            f32(2, 128, 128),
            f32(4, 3, 16, 128),
            f32(4, 16, 128),
            f32(3, 2, 16, 128),
            f32(3, 2, 8, 128),
            f32(3, 2, 8, 128),
            f32(3, 4, 16, 128),
            f32(2, 4, 16, 128),
            f32(2, 128, 128),
            f32(16, 2048),
            f32(16, 128),
            f32(16, 128),
            f32(3, 16, 128),
            f32(3, 16, 128),
            f32(3, 1, 16, 128),
            f32(7, 1, 16, 128),
            f32(3, 2, 16, 128),
            f32(7, 2, 16, 128),
            f32(16, 128),
            f32(16, 1, 128),
            f32(16, 8, 128),
            bf16(2, 49, 16, 128),
            bf16(FAR, 2, 16, 256),
            bf16(PLANE, 2, 16, 256),
            pltpu.SemaphoreType.DMA((48,)),
            pltpu.SemaphoreType.DMA((48,)),
        ],
        compiler_params=pltpu.CompilerParams(
            collective_id=0, has_side_effects=True, vmem_limit_bytes=67043328
        ),
        name="green_step",
    )(orbitals, points, quad_weight, external, screening, level_index, near_cells)


def solution(mesh):
    in_specs = (
        P("orb", "space", None),
        P(None, "space", None),
        P("space", None),
        P("space", None),
        P(),
        P("orb"),
        P("space", None),
        P("space", None),
    )
    out_specs = (P("orb", "space", None), P("space", None))
    return jax.shard_map(body, mesh=mesh, in_specs=in_specs, out_specs=out_specs, check_vma=False)
```

```python
import functools
import math

import jax
import jax.numpy as jnp
from jax import lax
from jax.experimental import pallas as pl
from jax.experimental.pallas import tpu as pltpu
from jax.sharding import PartitionSpec as P

F32 = jnp.float32
BF16 = jnp.bfloat16
HI = lax.Precision.HIGHEST
LANES = (((1,), (1,)), ((), ()))
SOFTEN = 6.25e-06
SCALE = -0.5 / math.pi
SIDE = 0.25
NODE = [math.cos((2 * a + 1) * math.pi / 8) for a in range(4)]
OFFSET = [0.5 * (t + 1.0) for t in NODE]
FAR = 12
PLANE = 8
DENSE = FAR + PLANE
NEAR = 4 * 4 + 8 * 6 + 4 * 9


def iota(shape, axis):
    return lax.broadcasted_iota(jnp.int32, shape, axis)


def pick(index, table):
    out = jnp.full(index.shape, table[0], F32)
    for i in range(1, 4):
        out = jnp.where(index == i, F32(table[i]), out)
    return out


def pick_scalar(index, table):
    out = F32(table[0])
    for i in range(1, 4):
        out = jnp.where(index == i, F32(table[i]), out)
    return out


def select_rows(row, parts):
    out = jnp.where(row == 0, parts[0], parts[1])
    for i in range(2, 4):
        out = jnp.where(row == i, parts[i], out)
    return out


def lagrange(u):
    out = []
    for a in range(4):
        term = None
        for n in range(4):
            if n != a:
                factor = (u - NODE[n]) * (1.0 / (NODE[a] - NODE[n]))
                term = factor if term is None else term * factor
        out.append(term)
    return out


def near_count(t):
    cx, cy = t % 4, t // 4
    nx = jnp.where((cx == 0) | (cx == 3), 2, 3)
    ny = jnp.where((cy == 0) | (cy == 3), 2, 3)
    return 3 * nx * ny


def kernel(
    orb, pts, qw, ext, screening, level, near, out, hart,
    G, GN, ACC, TB, DXY, PR, CV, SV, MC, MS, LG, LP, A, AP, D0, D1, RA, RB,
    ZCO, ZCR, ZSO, ZSR, ZF, HG, FM, send, recv,
):
    o = lax.axis_index("orb")
    g = lax.axis_index("space")
    core, x, y = g % 2, g // 2 % 4, g // 8
    zi, zb = o % 4, o // 4
    up, down = (g + 1) % 32, (g + 31) % 32
    lane = iota((1, 128), 1)

    def other_z(d):
        return {"orb": (o + d) % 16}

    def other_x(d):
        return {"space": g + 2 * ((x + d) % 4 - x)}

    def other_y(d):
        return {"space": g + 8 * ((y + d) % 4 - y)}

    barrier = pltpu.get_barrier_semaphore()
    partners = [other_z(d) for d in range(1, 16)]
    partners += [other_x(d) for d in range(1, 4)] + [other_y(d) for d in range(1, 4)]
    partners += [{"space": up}, {"space": down}]
    for partner in partners:
        pl.semaphore_signal(barrier, inc=1, device_id=partner, device_id_type=pl.DeviceIdType.MESH)

    def copy(src, dst, i, device, j=None):
        return pltpu.make_async_remote_copy(
            src, dst, send.at[i], recv.at[i if j is None else j],
            device_id=device, device_id_type=pl.DeviceIdType.MESH,
        )

    def rim(ref, i):
        return [
            copy(ref.at[1], ref.at[0], i, {"space": up}),
            copy(ref.at[1], ref.at[2], i + 1, {"space": down}),
        ]

    def begin(copies):
        for c in copies:
            c.start()

    def finish(copies):
        for c in copies:
            c.wait()

    rates = [-screening[level[v]] * (1.0 / math.log(2.0)) for v in range(2)]

    def columns(t):
        for k in range(3):
            TB[k] = jnp.broadcast_to(pts[k, pl.ds(t, 1), :], (128, 128)).T

    def green(r2):
        inv = lax.rsqrt(r2)
        s = r2 * inv
        return [(jnp.exp2(s * rate) * inv).astype(BF16) for rate in rates]

    def far_xy():
        a, b, c8 = lane // 4 % 4, lane % 4, lane // 16
        gx = (c8 % 4).astype(F32) * SIDE + SIDE * pick(a, OFFSET)
        dx = TB[0] - gx
        for half in range(2):
            gy = (c8 // 4 + 2 * half).astype(F32) * SIDE + SIDE * pick(b, OFFSET)
            dy = TB[1] - gy
            DXY[half] = dx * dx + (dy * dy + SOFTEN)

    def plane_z():
        gz = (lane // 4).astype(F32) * SIDE + SIDE * pick(lane % 4, OFFSET)
        dz = TB[2] - gz
        DXY[0] = dz * dz + SOFTEN

    def far_dz2(k):
        dz = TB[2] - ((g - 1 + k // 4).astype(F32) * SIDE + SIDE * pick_scalar(k % 4, OFFSET))
        return dz * dz

    def plane_xy2(ab):
        dx = TB[0] - pick_scalar(ab // 4, OFFSET)
        dy = TB[1] - pick_scalar(ab % 4, OFFSET)
        return dx * dx + dy * dy

    def store_green(block, half, r2):
        for v, values in enumerate(green(r2)):
            G[block, v, :, half * 128 : half * 128 + 128] = values

    def dense(lo, hi):
        def cell(t, carry):
            columns(t)
            far_xy()

            def far(j, c):
                for k in (2 * j, 2 * j + 1):
                    dz2 = far_dz2(k)
                    for half in range(2):
                        store_green(t * DENSE + k, half, DXY[half] + dz2)
                return c

            lax.fori_loop(0, FAR // 2, far, 0)
            plane_z()

            def planes(j, c):
                for k in (2 * j, 2 * j + 1):
                    for half in range(2):
                        store_green(t * DENSE + FAR + k, half, plane_xy2(2 * k + half) + DXY[0])
                return c

            lax.fori_loop(0, PLANE // 2, planes, 0)
            return carry

        lax.fori_loop(lo, hi, cell, 0)

    def near_slot(t, n):
        cell = near[t, n]
        return jnp.where(cell >= 0, jnp.clip(cell - 16 * (g - 1), 0, 47), 48)

    def near_r2(slot):
        lev, c = slot // 16, slot % 16
        total = None
        for k in range(3):
            d = TB[k] - PR[lev, k, pl.ds(c, 1), :]
            total = d * d + SOFTEN if total is None else total + d * d
        return total

    def near_green(lo, hi, off):
        def cell(t, off):
            columns(t)
            count = near_count(t) // 3

            def triple(p, c):
                for i in range(3):
                    for v, values in enumerate(green(near_r2(near_slot(t, 3 * p + i)))):
                        GN[off + p, v, i] = values
                return c

            lax.fori_loop(0, count, triple, 0)
            return off + count

        return lax.fori_loop(lo, hi, cell, off)

    D0[...] = 2.0 * (orb[0] * orb[0] + orb[1] * orb[1])
    PR[1] = pts[...]
    PR[3] = jnp.zeros((3, 16, 128), F32)
    CV[3] = jnp.zeros((16, 128), F32)
    SV[3] = jnp.zeros((2, 16, 128), F32)
    row16 = iota((16, 128), 0)
    ux = (pts[0] - (row16 % 4).astype(F32) * SIDE) * (2.0 / SIDE) - 1.0
    uy = (pts[1] - (row16 // 4).astype(F32) * SIDE) * (2.0 / SIDE) - 1.0
    uz = (pts[2] - g.astype(F32) * SIDE) * (2.0 / SIDE) - 1.0
    for k, u in enumerate((ux, uy, uz)):
        for a, w in enumerate(lagrange(u)):
            LG[k, a] = w
    for k in range(2):
        for a, w in enumerate(lagrange(2.0 * pts[k] - 1.0)):
            LP[k, a] = w
    row8 = iota((8, 128), 0)
    for c in range(16):
        one = slice(c, c + 1)
        ycell = select_rows(row8 % 4, [LG[1, b, one, :] for b in range(4)])
        yplane = select_rows(row8 % 4, [LP[1, b, one, :] for b in range(4)])
        for k in range(2):
            xcell = jnp.where(row8 < 4, LG[0, 2 * k, one, :], LG[0, 2 * k + 1, one, :])
            xplane = jnp.where(row8 < 4, LP[0, 2 * k, one, :], LP[0, 2 * k + 1, one, :])
            at = c % 8 * 16 + k * 8
            A[c // 8, at : at + 8, :] = xcell * ycell
            AP[k * 8 : k * 8 + 8, c * 128 : c * 128 + 128] = xplane * yplane

    def masks(t, carry):
        lev = g - 1 + row8 // 2
        cell = lev * 16 + row8 % 2 * 8 + lane // 16
        hit = (lev < 0) | (lev > 31)
        for n in range(27):
            hit = hit | (cell == near[t, n])
        FM[t] = jnp.where(hit, 0.0, 1.0)
        return carry

    lax.fori_loop(0, 16, masks, 0)
    dense(0, 5)
    pl.semaphore_wait(barrier, len(partners))

    first = [copy(D0, RA.at[d - 1], d - 1, {"orb": zb * 4 + (zi + d) % 4}) for d in range(1, 4)]
    begin(first)
    edge_points = rim(PR, 6)
    begin(edge_points)
    dense(5, 8)
    finish(first)
    D1[...] = D0[...] + (RA[0] + RA[1]) + RA[2]
    second = [
        copy(D1, RB.at[d - 1], 2 + d, {"orb": (zb + d) % 4 * 4 + zi}) for d in range(1, 4)
    ]
    begin(second)
    dense(8, 14)
    finish(second)
    weight = qw[...] * (SIDE**3 / 128)
    CV[1] = weight * (D1[...] + (RB[0] + RB[1]) + RB[2])

    def moments(values, cells):
        tiles = []
        for c in range(16):
            one = slice(c, c + 1)
            z = select_rows(row8 % 4, [LG[2, d, one, :] for d in range(4)])
            parts = [v[one, :] for v in values]
            tiles.append(z * jnp.where(row8 < 4, parts[0], parts[1] if len(parts) > 1 else 0.0))
        for half in range(2):
            rows = jnp.concatenate(tiles[half * 8 : half * 8 + 8], axis=0)
            every = lax.dot_general(rows, A[half], LANES, precision=HI, preferred_element_type=F32)
            total = jnp.zeros((8, 128), F32)
            for c in range(8):
                total = jnp.where(lane // 16 == c, every[c * 8 : c * 8 + 8], total)
            cells[1, half] = total
        wide = jnp.concatenate(tiles, axis=1)
        small = lax.dot_general(AP[...], wide, LANES, precision=HI, preferred_element_type=F32)
        planes = []
        for v in range(len(values)):
            spread = (iota((8, 128), 0) == v * 4 + lane % 4).astype(F32)
            planes.append(jnp.dot(small, spread, precision=HI, preferred_element_type=F32))
        return planes

    def gather_planes(planes, own, got, base, fill):
        for v, plane in enumerate(planes):
            own[0, v] = plane
        stage = [copy(own.at[0], got.at[0], base, {"space": g + 1 - 2 * core})]
        begin(stage)
        fill[0]()
        finish(stage)
        own[1] = jnp.where(lane // 4 % 2 == core, own[0], got[0])
        stage = [copy(own.at[1], got.at[d], base + d, other_x(d)) for d in range(1, 4)]
        begin(stage)
        fill[1]()
        finish(stage)
        full = own[1]
        for d in range(1, 4):
            full = jnp.where(lane // 8 % 4 == (x + 4 - d) % 4, got[d], full)
        own[2] = full
        stage = [copy(own.at[2], got.at[3 + d], base + 3 + d, other_y(d)) for d in range(1, 4)]
        begin(stage)
        fill[2]()
        finish(stage)
        full = own[2]
        for d in range(1, 4):
            full = jnp.where(lane // 32 == (y + 4 - d) % 4, got[3 + d], full)
        return jnp.where(jnp.abs(lane // 4 - g) >= 2, full, 0.0)

    offset = [0]

    def more(lo, hi):
        offset[0] = near_green(lo, hi, offset[0])

    edge_charge = rim(CV, 8)
    begin(edge_charge)
    planes = moments([CV.at[1]], MC)
    edge_moments = rim(MC, 10)
    begin(edge_moments)
    finish(edge_points)
    full = gather_planes(
        planes, ZCO, ZCR, 12, [lambda: more(0, 2), lambda: dense(14, 16), lambda: more(2, 6)]
    )
    for v in range(1):
        ZF[v] = full[v]
    finish(edge_charge)
    finish(edge_moments)

    columns(o)
    acc = jnp.zeros((128, 128), F32)

    def near_hartree(p, acc):
        for i in range(3):
            slot = near_slot(o, 3 * p + i)
            acc = acc + lax.rsqrt(near_r2(slot)) * CV[slot // 16, pl.ds(slot % 16, 1), :]
        return acc

    acc = lax.fori_loop(0, near_count(o) // 3, near_hartree, acc)
    far_xy()

    def far_hartree(k, acc):
        dz2 = far_dz2(k)
        for half in range(2):
            row = MC[k // 4, half, pl.ds(k % 4, 1), :] * FM[o, pl.ds(k // 4 * 2 + half, 1), :]
            acc = acc + lax.rsqrt(DXY[half] + dz2) * row
        return acc

    acc = lax.fori_loop(0, FAR, far_hartree, acc)
    plane_z()

    def plane_hartree(k, acc):
        for half in range(2):
            ab = 2 * k + half
            acc = acc + lax.rsqrt(plane_xy2(ab) + DXY[0]) * ZF[0, pl.ds(ab, 1), :]
        return acc

    acc = lax.fori_loop(0, PLANE, plane_hartree, acc)
    HG[o] = jnp.sum(acc.T, axis=0, keepdims=True)
    shares = [copy(HG.at[o], HG.at[o], 18 + d, other_z(d), 19 + o) for d in range(1, 16)]
    begin(shares)
    more(6, 16)
    for d in range(1, 16):
        shares[d - 1].wait_send()
        k = (o + 16 - d) % 16
        copy(HG.at[k], HG.at[k], 18 + d, other_z(d), 19 + k).wait_recv()
    for c in range(16):
        hart[c : c + 1, :] = HG[c]

    scaled = weight * (ext[...] + hart[...])
    for v in range(2):
        SV[1, v] = scaled * orb[v]
    edge_sources = rim(SV, 35)
    begin(edge_sources)
    planes = moments([SV.at[1, 0], SV.at[1, 1]], MS)
    edge_moments = rim(MS, 37)
    begin(edge_moments)

    def local(lo, hi, off):
        def cell(t, off):
            def far(lev, acc):
                acc = list(acc)
                for half in range(2):
                    mask = FM[t, pl.ds(lev * 2 + half, 1), :]
                    for d in range(4):
                        for v in range(2):
                            r = v * 4 + d
                            row = MS[lev, half, r : r + 1, :] * mask
                            values = G[t * DENSE + lev * 4 + d, v, :, half * 128 : half * 128 + 128]
                            acc[v] = acc[v] + values.astype(F32) * row
                return tuple(acc)

            acc = lax.fori_loop(0, 3, far, (jnp.zeros((128, 128), F32),) * 2)
            count = near_count(t) // 3

            def triple(p, acc):
                acc = list(acc)
                for i in range(3):
                    slot = near_slot(t, 3 * p + i)
                    for v in range(2):
                        row = SV[slot // 16, v, pl.ds(slot % 16, 1), :]
                        acc[v] = acc[v] + GN[off + p, v, i].astype(F32) * row
                return tuple(acc)

            acc = lax.fori_loop(0, count, triple, acc)
            for v in range(2):
                ACC[t, v] = acc[v]
            return off + count

        return lax.fori_loop(lo, hi, cell, off)

    done = [0]

    def apply(lo, hi):
        done[0] = local(lo, hi, done[0])

    def arrived():
        finish(edge_sources)
        finish(edge_moments)
        apply(0, 5)

    full = gather_planes(
        planes, ZSO, ZSR, 39, [lambda: None, arrived, lambda: apply(5, 11)]
    )
    for v in range(2):
        ZF[v] = full[v]
    apply(11, 16)

    def update(t, carry):
        for v in range(2):
            acc = ACC[t, v]
            for k in range(PLANE):
                for half in range(2):
                    ab = 2 * k + half
                    values = G[t * DENSE + FAR + k, v, :, half * 128 : half * 128 + 128]
                    acc = acc + values.astype(F32) * ZF[v, ab : ab + 1, :]
            out[v, pl.ds(t, 1), :] = SCALE * jnp.sum(acc.T, axis=0, keepdims=True)
        return carry

    lax.fori_loop(0, 16, update, 0)


def body(orbitals, points, quad_weight, external, screening, level_index, near_cells, far_cells):
    vmem = pl.BlockSpec(memory_space=pltpu.VMEM)
    smem = pl.BlockSpec(memory_space=pltpu.SMEM)

    def f32(*shape):
        return pltpu.VMEM(shape, F32)

    def bf16(*shape):
        return pltpu.VMEM(shape, BF16)

    return pl.pallas_call(
        kernel,
        out_shape=(
            jax.ShapeDtypeStruct((2, 16, 128), F32),
            jax.ShapeDtypeStruct((16, 128), F32),
        ),
        in_specs=[vmem] * 4 + [smem] * 3,
        out_specs=(vmem, vmem),
        scratch_shapes=[
            bf16(16 * DENSE, 2, 128, 256),
            bf16(NEAR, 2, 3, 128, 128),
            f32(16, 2, 128, 128),
            f32(3, 128, 128),
            f32(2, 128, 128),
            f32(4, 3, 16, 128),
            f32(4, 16, 128),
            f32(4, 2, 16, 128),
            f32(3, 2, 8, 128),
            f32(3, 2, 8, 128),
            f32(3, 4, 16, 128),
            f32(2, 4, 16, 128),
            f32(2, 128, 128),
            f32(16, 2048),
            f32(16, 128),
            f32(16, 128),
            f32(3, 16, 128),
            f32(3, 16, 128),
            f32(3, 1, 16, 128),
            f32(7, 1, 16, 128),
            f32(3, 2, 16, 128),
            f32(7, 2, 16, 128),
            f32(2, 16, 128),
            f32(16, 1, 128),
            f32(16, 8, 128),
            pltpu.SemaphoreType.DMA((48,)),
            pltpu.SemaphoreType.DMA((48,)),
        ],
        compiler_params=pltpu.CompilerParams(
            collective_id=0, has_side_effects=True, vmem_limit_bytes=67043328
        ),
        name="green_step",
    )(orbitals, points, quad_weight, external, screening, level_index, near_cells)


def solution(mesh):
    in_specs = (
        P("orb", "space", None),
        P(None, "space", None),
        P("space", None),
        P("space", None),
        P(),
        P("orb"),
        P("space", None),
        P("space", None),
    )
    out_specs = (P("orb", "space", None), P("space", None))
    return jax.shard_map(body, mesh=mesh, in_specs=in_specs, out_specs=out_specs, check_vma=False)
```

```python
import functools
import math

import jax
import jax.numpy as jnp
from jax import lax
from jax.experimental import pallas as pl
from jax.experimental.pallas import tpu as pltpu
from jax.sharding import PartitionSpec as P

F32 = jnp.float32
BF16 = jnp.bfloat16
HI = lax.Precision.HIGHEST
LANES = (((1,), (1,)), ((), ()))
SOFTEN = 6.25e-06
SCALE = -0.5 / math.pi
SIDE = 0.25
NODE = [math.cos((2 * a + 1) * math.pi / 8) for a in range(4)]
OFFSET = [0.5 * (t + 1.0) for t in NODE]
FAR = 24
PLANE = 16
DENSE = FAR + PLANE
NEAR = 4 * 4 + 8 * 6 + 4 * 9


def iota(shape, axis):
    return lax.broadcasted_iota(jnp.int32, shape, axis)


def pick(index, table):
    out = jnp.full(index.shape, table[0], F32)
    for i in range(1, 4):
        out = jnp.where(index == i, F32(table[i]), out)
    return out


def pick_scalar(index, table):
    out = F32(table[0])
    for i in range(1, 4):
        out = jnp.where(index == i, F32(table[i]), out)
    return out


def select_rows(row, parts):
    out = jnp.where(row == 0, parts[0], parts[1])
    for i in range(2, 4):
        out = jnp.where(row == i, parts[i], out)
    return out


def lagrange(u):
    out = []
    for a in range(4):
        term = None
        for n in range(4):
            if n != a:
                factor = (u - NODE[n]) * (1.0 / (NODE[a] - NODE[n]))
                term = factor if term is None else term * factor
        out.append(term)
    return out


def near_count(t):
    cx, cy = t % 4, t // 4
    nx = jnp.where((cx == 0) | (cx == 3), 2, 3)
    ny = jnp.where((cy == 0) | (cy == 3), 2, 3)
    return 3 * nx * ny


def kernel(
    orb, pts, qw, ext, screening, level, near, out, hart,
    G, GN, ACC, TB, DXY, PR, CV, SV, MC, MS, LG, LP, A, AP, D0, RA,
    QC, RC, QS, RS, ZF, HG, FM, send, recv,
):
    o = lax.axis_index("orb")
    g = lax.axis_index("space")
    up, down = (g + 1) % 32, (g + 31) % 32
    lane = iota((1, 128), 1)
    away = lane // 8 + 16 * (lane // 4 % 2)
    level_of = (g + 32 - away) % 32

    def other_z(d):
        return {"orb": (o + d) % 16}

    def other_g(d):
        return {"space": (g + d) % 32}

    barrier = pltpu.get_barrier_semaphore()
    partners = [other_z(d) for d in range(1, 16)]
    partners += [other_g(d) for d in range(1, 32)]
    for partner in partners:
        pl.semaphore_signal(barrier, inc=1, device_id=partner, device_id_type=pl.DeviceIdType.MESH)

    def copy(src, dst, i, device):
        return pltpu.make_async_remote_copy(
            src, dst, send.at[i], recv.at[i],
            device_id=device, device_id_type=pl.DeviceIdType.MESH,
        )

    def all_of(ref, i, device):
        whole = copy(ref, ref, i, device)
        whole.wait_send()
        whole.wait_recv()

    def rim(ref, i):
        return [
            copy(ref.at[1], ref.at[0], i, {"space": up}),
            copy(ref.at[1], ref.at[2], i + 1, {"space": down}),
        ]

    def begin(copies):
        for c in copies:
            c.start()

    def finish(copies):
        for c in copies:
            c.wait()

    rates = [-screening[level[v]] * (1.0 / math.log(2.0)) for v in range(2)]

    def columns(t):
        for k in range(3):
            TB[k] = jnp.broadcast_to(pts[k, pl.ds(t, 1), :], (128, 128)).T

    def green(r2):
        inv = lax.rsqrt(r2)
        s = r2 * inv
        return [(jnp.exp2(s * rate) * inv).astype(BF16) for rate in rates]

    def far_xy():
        a, b, c8 = lane // 4 % 4, lane % 4, lane // 16
        gx = (c8 % 4).astype(F32) * SIDE + SIDE * pick(a, OFFSET)
        dx = TB[0] - gx
        for half in range(2):
            gy = (c8 // 4 + 2 * half).astype(F32) * SIDE + SIDE * pick(b, OFFSET)
            dy = TB[1] - gy
            DXY[half] = dx * dx + (dy * dy + SOFTEN)

    def plane_z():
        gz = level_of.astype(F32) * SIDE + SIDE * pick(lane % 4, OFFSET)
        dz = TB[2] - gz
        DXY[0] = dz * dz + SOFTEN
        for b in range(4):
            dy = TB[1] - OFFSET[b]
            DXY[1 + b] = dy * dy

    def far_dz2(lev, d):
        dz = TB[2] - ((g - 1 + lev).astype(F32) * SIDE + SIDE * OFFSET[d])
        return dz * dz

    def plane_xz2(a):
        dx = TB[0] - pick_scalar(a, OFFSET)
        return dx * dx + DXY[0]

    def store_green(block, r2):
        for v, values in enumerate(green(r2)):
            G[block, v] = values

    def dense(lo, hi):
        def cell(t, carry):
            columns(t)
            far_xy()

            def far(lev, c):
                for d in range(4):
                    dz2 = far_dz2(lev, d)
                    for half in range(2):
                        store_green(t * DENSE + lev * 8 + d * 2 + half, DXY[half] + dz2)
                return c

            lax.fori_loop(0, 3, far, 0)
            plane_z()

            def planes(a, c):
                xz2 = plane_xz2(a)
                for b in range(4):
                    store_green(t * DENSE + FAR + a * 4 + b, xz2 + DXY[1 + b])
                return c

            lax.fori_loop(0, 4, planes, 0)
            return carry

        lax.fori_loop(lo, hi, cell, 0)

    def near_slot(t, n):
        cell = near[t, n]
        return jnp.where(cell >= 0, jnp.clip(cell - 16 * (g - 1), 0, 47), 48)

    def near_r2(slot):
        lev, c = slot // 16, slot % 16
        total = None
        for k in range(3):
            d = TB[k] - PR[lev, k, pl.ds(c, 1), :]
            total = d * d + SOFTEN if total is None else total + d * d
        return total

    def near_green(lo, hi, off):
        def cell(t, off):
            columns(t)
            count = near_count(t) // 3

            def triple(p, c):
                for i in range(3):
                    for v, values in enumerate(green(near_r2(near_slot(t, 3 * p + i)))):
                        GN[off + p, v, i] = values
                return c

            lax.fori_loop(0, count, triple, 0)
            return off + count

        return lax.fori_loop(lo, hi, cell, off)

    D0[...] = 2.0 * (orb[0] * orb[0] + orb[1] * orb[1])
    PR[1] = pts[...]
    PR[3] = jnp.zeros((3, 16, 128), F32)
    CV[3] = jnp.zeros((16, 128), F32)
    SV[3] = jnp.zeros((2, 16, 128), F32)
    row16 = iota((16, 128), 0)
    ux = (pts[0] - (row16 % 4).astype(F32) * SIDE) * (2.0 / SIDE) - 1.0
    uy = (pts[1] - (row16 // 4).astype(F32) * SIDE) * (2.0 / SIDE) - 1.0
    uz = (pts[2] - g.astype(F32) * SIDE) * (2.0 / SIDE) - 1.0
    for k, u in enumerate((ux, uy, uz)):
        for a, w in enumerate(lagrange(u)):
            LG[k, a] = w
    for k in range(2):
        for a, w in enumerate(lagrange(2.0 * pts[k] - 1.0)):
            LP[k, a] = w
    row8 = iota((8, 128), 0)
    for c in range(16):
        one = slice(c, c + 1)
        ycell = select_rows(row8 % 4, [LG[1, b, one, :] for b in range(4)])
        yplane = select_rows(row8 % 4, [LP[1, b, one, :] for b in range(4)])
        for k in range(2):
            xcell = jnp.where(row8 < 4, LG[0, 2 * k, one, :], LG[0, 2 * k + 1, one, :])
            xplane = jnp.where(row8 < 4, LP[0, 2 * k, one, :], LP[0, 2 * k + 1, one, :])
            at = c % 8 * 16 + k * 8
            A[c // 8, at : at + 8, :] = xcell * ycell
            AP[k * 8 : k * 8 + 8, c * 128 : c * 128 + 128] = xplane * yplane

    def masks(t, carry):
        lev = g - 1 + row8 // 2
        cell = lev * 16 + row8 % 2 * 8 + lane // 16
        hit = (lev < 0) | (lev > 31)
        for n in range(27):
            hit = hit | (cell == near[t, n])
        FM[t] = jnp.where(hit, 0.0, 1.0)
        return carry

    lax.fori_loop(0, 16, masks, 0)
    dense(0, 5)
    pl.semaphore_wait(barrier, len(partners))

    spread = [copy(D0, RA.at[d - 1], 0, other_z(d)) for d in range(1, 16)]
    begin(spread)
    edge_points = rim(PR, 1)
    begin(edge_points)
    dense(5, 14)
    all_of(RA, 0, other_z(1))
    total = D0[...]
    for d in range(15):
        total = total + RA[d]
    weight = qw[...] * (SIDE**3 / 128)
    CV[1] = weight * total

    def moments(values, cells):
        tiles = []
        for c in range(16):
            one = slice(c, c + 1)
            z = select_rows(row8 % 4, [LG[2, d, one, :] for d in range(4)])
            parts = [v[one, :] for v in values]
            tiles.append(z * jnp.where(row8 < 4, parts[0], parts[1] if len(parts) > 1 else 0.0))
        for half in range(2):
            rows = jnp.concatenate(tiles[half * 8 : half * 8 + 8], axis=0)
            every = lax.dot_general(rows, A[half], LANES, precision=HI, preferred_element_type=F32)
            total = jnp.zeros((8, 128), F32)
            for c in range(8):
                total = jnp.where(lane // 16 == c, every[c * 8 : c * 8 + 8], total)
            cells[1, half] = total
        wide = jnp.concatenate(tiles, axis=1)
        return lax.dot_general(wide, AP[...], LANES, precision=HI, preferred_element_type=F32)

    def send_planes(small, own, got, i):
        own[...] = jnp.zeros((8, 128), F32)
        own[:, 0:16] = small
        got[0] = own[...]
        begin([copy(own, got.at[d], i, other_g(d)) for d in range(1, 32)])

    def take_planes(got, i, count):
        all_of(got.at[1:32], i, other_g(1))
        low = got[0:16].reshape(128, 128).T[0:16]
        high = got[16:32].reshape(128, 128).T[0:16]
        first = lane // 4 % 2 == 0
        parts = [jnp.where(first, low, pltpu.roll(high, 4, 1))]
        if count == 2:
            parts.append(jnp.where(first, pltpu.roll(low, 124, 1), high))
        for v, part in enumerate(parts):
            ZF[v] = jnp.where(jnp.abs(level_of - g) >= 2, part, 0.0)

    offset = [0]

    def more(lo, hi):
        offset[0] = near_green(lo, hi, offset[0])

    edge_charge = rim(CV, 3)
    begin(edge_charge)
    small = moments([CV.at[1]], MC)
    edge_moments = rim(MC, 5)
    begin(edge_moments)
    send_planes(small, QC, RC, 7)
    dense(14, 16)
    finish(edge_points)
    more(0, 1)
    finish(edge_charge)
    finish(edge_moments)

    columns(o)
    acc = jnp.zeros((128, 128), F32)

    def near_hartree(p, acc):
        for i in range(3):
            slot = near_slot(o, 3 * p + i)
            acc = acc + lax.rsqrt(near_r2(slot)) * CV[slot // 16, pl.ds(slot % 16, 1), :]
        return acc

    acc = lax.fori_loop(0, near_count(o) // 3, near_hartree, acc)
    far_xy()

    def far_hartree(lev, acc):
        for half in range(2):
            mask = FM[o, pl.ds(lev * 2 + half, 1), :]
            for d in range(4):
                row = MC[lev, half, d : d + 1, :] * mask
                acc = acc + lax.rsqrt(DXY[half] + far_dz2(lev, d)) * row
        return acc

    acc = lax.fori_loop(0, 3, far_hartree, acc)
    plane_z()
    take_planes(RC, 7, 1)

    def plane_hartree(a, acc):
        xz2 = plane_xz2(a)
        for b in range(4):
            acc = acc + lax.rsqrt(xz2 + DXY[1 + b]) * ZF[0, pl.ds(a * 4 + b, 1), :]
        return acc

    acc = lax.fori_loop(0, 4, plane_hartree, acc)
    HG[0] = jnp.sum(acc.T, axis=0, keepdims=True)
    begin([copy(HG.at[0], HG.at[d], 8, other_z(d)) for d in range(1, 16)])
    more(1, 11)
    all_of(HG.at[1:16], 8, other_z(1))
    for d in range(16):
        hart[pl.ds((o + 16 - d) % 16, 1), :] = HG[d]

    scaled = weight * (ext[...] + hart[...])
    for v in range(2):
        SV[1, v] = scaled * orb[v]
    edge_sources = rim(SV, 9)
    begin(edge_sources)
    small = moments([SV.at[1, 0], SV.at[1, 1]], MS)
    edge_moments = rim(MS, 11)
    begin(edge_moments)
    send_planes(small, QS, RS, 13)
    more(11, 16)

    def weigh(values, rows):
        total = None
        for value, row in zip(values, rows):
            wide = jnp.broadcast_to(row, (16, 128)).astype(BF16)
            term = value.reshape(8, 16, 128) * wide[None]
            total = term if total is None else total + term
        return total.astype(F32)

    def local(lo, hi, off):
        def cell(t, off):
            def far(lev, acc):
                acc = list(acc)
                masks = [FM[t, pl.ds(lev * 2 + half, 1), :] for half in range(2)]
                for d in range(4):
                    for v in range(2):
                        r = v * 4 + d
                        at = t * DENSE + lev * 8 + d * 2
                        acc[v] = acc[v] + weigh(
                            [G[at, v], G[at + 1, v]],
                            [MS[lev, half, r : r + 1, :] * masks[half] for half in range(2)],
                        )
                return tuple(acc)

            acc = lax.fori_loop(0, 3, far, (jnp.zeros((8, 16, 128), F32),) * 2)
            acc = tuple(a.reshape(128, 128) for a in acc)
            count = near_count(t) // 3

            def triple(p, acc):
                acc = list(acc)
                for i in range(3):
                    slot = near_slot(t, 3 * p + i)
                    for v in range(2):
                        row = SV[slot // 16, v, pl.ds(slot % 16, 1), :]
                        acc[v] = acc[v] + GN[off + p, v, i].astype(F32) * row
                return tuple(acc)

            acc = lax.fori_loop(0, count, triple, acc)
            for v in range(2):
                ACC[t, v] = acc[v]
            return off + count

        return lax.fori_loop(lo, hi, cell, off)

    done = [0]

    def apply(lo, hi):
        done[0] = local(lo, hi, done[0])

    finish(edge_sources)
    finish(edge_moments)
    apply(0, 16)
    take_planes(RS, 13, 2)

    def update(t, carry):
        for v in range(2):
            acc = ACC[t, v]
            acc = acc.reshape(8, 16, 128)
            for ab in range(0, PLANE, 2):
                at = t * DENSE + FAR + ab
                acc = acc + weigh(
                    [G[at, v], G[at + 1, v]], [ZF[v, ab : ab + 1, :], ZF[v, ab + 1 : ab + 2, :]]
                )
            acc = acc.reshape(128, 128)
            out[v, pl.ds(t, 1), :] = SCALE * jnp.sum(acc.T, axis=0, keepdims=True)
        return carry

    lax.fori_loop(0, 16, update, 0)


def body(orbitals, points, quad_weight, external, screening, level_index, near_cells, far_cells):
    vmem = pl.BlockSpec(memory_space=pltpu.VMEM)
    smem = pl.BlockSpec(memory_space=pltpu.SMEM)

    def f32(*shape):
        return pltpu.VMEM(shape, F32)

    def bf16(*shape):
        return pltpu.VMEM(shape, BF16)

    return pl.pallas_call(
        kernel,
        out_shape=(
            jax.ShapeDtypeStruct((2, 16, 128), F32),
            jax.ShapeDtypeStruct((16, 128), F32),
        ),
        in_specs=[vmem] * 4 + [smem] * 3,
        out_specs=(vmem, vmem),
        scratch_shapes=[
            bf16(16 * DENSE, 2, 128, 128),
            bf16(NEAR, 2, 3, 128, 128),
            f32(16, 2, 128, 128),
            f32(3, 128, 128),
            f32(5, 128, 128),
            f32(4, 3, 16, 128),
            f32(4, 16, 128),
            f32(4, 2, 16, 128),
            f32(3, 2, 8, 128),
            f32(3, 2, 8, 128),
            f32(3, 4, 16, 128),
            f32(2, 4, 16, 128),
            f32(2, 128, 128),
            f32(16, 2048),
            f32(16, 128),
            f32(15, 16, 128),
            f32(8, 128),
            f32(32, 8, 128),
            f32(8, 128),
            f32(32, 8, 128),
            f32(2, 16, 128),
            f32(16, 1, 128),
            f32(16, 8, 128),
            pltpu.SemaphoreType.DMA((14,)),
            pltpu.SemaphoreType.DMA((14,)),
        ],
        compiler_params=pltpu.CompilerParams(
            collective_id=0, has_side_effects=True, vmem_limit_bytes=67043328
        ),
        name="green_step",
    )(orbitals, points, quad_weight, external, screening, level_index, near_cells)


def solution(mesh):
    in_specs = (
        P("orb", "space", None),
        P(None, "space", None),
        P("space", None),
        P("space", None),
        P(),
        P("orb"),
        P("space", None),
        P("space", None),
    )
    out_specs = (P("orb", "space", None), P("space", None))
    return jax.shard_map(body, mesh=mesh, in_specs=in_specs, out_specs=out_specs, check_vma=False)
```

```python
import functools
import math

import jax
import jax.numpy as jnp
from jax import lax
from jax.experimental import pallas as pl
from jax.experimental.pallas import tpu as pltpu
from jax.sharding import PartitionSpec as P

F32 = jnp.float32
BF16 = jnp.bfloat16
HI = lax.Precision.HIGHEST
LANES = (((1,), (1,)), ((), ()))
SOFTEN = 6.25e-06
SCALE = -0.5 / math.pi
SIDE = 0.25
NODE = [math.cos((2 * a + 1) * math.pi / 8) for a in range(4)]
OFFSET = [0.5 * (t + 1.0) for t in NODE]
FAR = 24
NEAR = 4 * 2 + 8 * 3 + 4 * 5


def iota(shape, axis):
    return lax.broadcasted_iota(jnp.int32, shape, axis)


def pick(index, table):
    out = jnp.full(index.shape, table[0], F32)
    for i in range(1, 4):
        out = jnp.where(index == i, F32(table[i]), out)
    return out


def pick_scalar(index, table):
    out = F32(table[0])
    for i in range(1, 4):
        out = jnp.where(index == i, F32(table[i]), out)
    return out


def select_rows(row, parts):
    out = jnp.where(row == 0, parts[0], parts[1])
    for i in range(2, 4):
        out = jnp.where(row == i, parts[i], out)
    return out


def lagrange(u):
    out = []
    for a in range(4):
        term = None
        for n in range(4):
            if n != a:
                factor = (u - NODE[n]) * (1.0 / (NODE[a] - NODE[n]))
                term = factor if term is None else term * factor
        out.append(term)
    return out


def near_count(t):
    cx, cy = t % 4, t // 4
    nx = jnp.where((cx == 0) | (cx == 3), 2, 3)
    ny = jnp.where((cy == 0) | (cy == 3), 2, 3)
    return 3 * nx * ny


def kernel(
    orb, pts, qw, ext, screening, level, near, out, hart,
    G, GN, ACC, TB, DXY, PR, CV, SV, MC, MS, LG, LP, A, AP, D0, RA,
    QC, RC, QS, RS, ZF, HG, FM, send, recv,
):
    o = lax.axis_index("orb")
    g = lax.axis_index("space")
    up, down = (g + 1) % 32, (g + 31) % 32
    lane = iota((1, 128), 1)
    away = lane // 8 + 16 * (lane // 4 % 2)
    level_of = (g + 32 - away) % 32

    def other_z(d):
        return {"orb": (o + d) % 16}

    def other_g(d):
        return {"space": (g + d) % 32}

    barrier = pltpu.get_barrier_semaphore()
    partners = [other_z(d) for d in range(1, 16)]
    partners += [other_g(d) for d in range(1, 32)]
    for partner in partners:
        pl.semaphore_signal(barrier, inc=1, device_id=partner, device_id_type=pl.DeviceIdType.MESH)

    def copy(src, dst, i, device):
        return pltpu.make_async_remote_copy(
            src, dst, send.at[i], recv.at[i],
            device_id=device, device_id_type=pl.DeviceIdType.MESH,
        )

    def all_of(ref, i, device):
        whole = copy(ref, ref, i, device)
        whole.wait_send()
        whole.wait_recv()

    def rim(ref, i):
        return [
            copy(ref.at[1], ref.at[0], i, {"space": up}),
            copy(ref.at[1], ref.at[2], i + 1, {"space": down}),
        ]

    def begin(copies):
        for c in copies:
            c.start()

    def finish(copies):
        for c in copies:
            c.wait()

    rates = [-screening[level[v]] * (1.0 / math.log(2.0)) for v in range(2)]

    def columns(t, carry):
        for k in range(3):
            TB[t, k] = jnp.broadcast_to(pts[k, pl.ds(t, 1), :], (128, 128)).T
        return carry

    def green(r2):
        inv = lax.rsqrt(r2)
        s = r2 * inv
        return [(jnp.exp2(s * rate) * inv).astype(BF16) for rate in rates]

    def far_xy(t):
        a, b, c8 = lane // 4 % 4, lane % 4, lane // 16
        gx = (c8 % 4).astype(F32) * SIDE + SIDE * pick(a, OFFSET)
        dx = TB[t, 0] - gx
        for half in range(2):
            gy = (c8 // 4 + 2 * half).astype(F32) * SIDE + SIDE * pick(b, OFFSET)
            dy = TB[t, 1] - gy
            DXY[half] = dx * dx + (dy * dy + SOFTEN)

    def plane_z(t):
        gz = level_of.astype(F32) * SIDE + SIDE * pick(lane % 4, OFFSET)
        dz = TB[t, 2] - gz
        DXY[0] = dz * dz + SOFTEN
        for b in range(4):
            dy = TB[t, 1] - OFFSET[b]
            DXY[1 + b] = dy * dy

    def far_dz2(t, lev, d):
        dz = TB[t, 2] - ((g - 1 + lev).astype(F32) * SIDE + SIDE * OFFSET[d])
        return dz * dz

    def plane_xz2(t, a):
        dx = TB[t, 0] - pick_scalar(a, OFFSET)
        return dx * dx + DXY[0]

    def store_green(block, r2):
        for v, values in enumerate(green(r2)):
            G[block, v] = values

    def dense(lo, hi):
        def cell(t, carry):
            far_xy(t)

            def far(lev, c):
                for d in range(4):
                    dz2 = far_dz2(t, lev, d)
                    for half in range(2):
                        store_green(t * FAR + lev * 8 + d * 2 + half, DXY[half] + dz2)
                return c

            lax.fori_loop(0, 3, far, 0)
            return carry

        lax.fori_loop(lo, hi, cell, 0)

    def near_slot(t, n):
        cell = near[t, jnp.minimum(n, 26)]
        live = (cell >= 0) & (n < 27)
        return jnp.where(live, jnp.clip(cell - 16 * (g - 1), 0, 47), 48)

    def near_r2(t, slot):
        lev, c = slot // 16, slot % 16
        total = None
        for k in range(3):
            d = TB[t, k] - PR[lev, k, pl.ds(c, 1), :]
            total = d * d + SOFTEN if total is None else total + d * d
        return total

    def near_green(lo, hi, off):
        def cell(t, off):
            count = (near_count(t) + 5) // 6

            def six(p, c):
                for i in range(6):
                    for v, values in enumerate(green(near_r2(t, near_slot(t, 6 * p + i)))):
                        GN[off + p, v, i] = values
                return c

            lax.fori_loop(0, count, six, 0)
            return off + count

        return lax.fori_loop(lo, hi, cell, off)

    D0[...] = 2.0 * (orb[0] * orb[0] + orb[1] * orb[1])
    PR[1] = pts[...]
    PR[3] = jnp.zeros((3, 16, 128), F32)
    CV[3] = jnp.zeros((16, 128), F32)
    SV[3] = jnp.zeros((2, 16, 128), F32)
    row16 = iota((16, 128), 0)
    ux = (pts[0] - (row16 % 4).astype(F32) * SIDE) * (2.0 / SIDE) - 1.0
    uy = (pts[1] - (row16 // 4).astype(F32) * SIDE) * (2.0 / SIDE) - 1.0
    uz = (pts[2] - g.astype(F32) * SIDE) * (2.0 / SIDE) - 1.0
    for k, u in enumerate((ux, uy, uz)):
        for a, w in enumerate(lagrange(u)):
            LG[k, a] = w
    for k in range(2):
        for a, w in enumerate(lagrange(2.0 * pts[k] - 1.0)):
            LP[k, a] = w
    row8 = iota((8, 128), 0)
    for c in range(16):
        one = slice(c, c + 1)
        ycell = select_rows(row8 % 4, [LG[1, b, one, :] for b in range(4)])
        yplane = select_rows(row8 % 4, [LP[1, b, one, :] for b in range(4)])
        for k in range(2):
            xcell = jnp.where(row8 < 4, LG[0, 2 * k, one, :], LG[0, 2 * k + 1, one, :])
            xplane = jnp.where(row8 < 4, LP[0, 2 * k, one, :], LP[0, 2 * k + 1, one, :])
            at = c % 8 * 16 + k * 8
            A[c // 8, at : at + 8, :] = xcell * ycell
            AP[k * 8 : k * 8 + 8, c * 128 : c * 128 + 128] = xplane * yplane

    def masks(t, carry):
        lev = g - 1 + row8 // 2
        cell = lev * 16 + row8 % 2 * 8 + lane // 16
        hit = (lev < 0) | (lev > 31)
        for n in range(27):
            hit = hit | (cell == near[t, n])
        FM[t] = jnp.where(hit, 0.0, 1.0)
        return carry

    lax.fori_loop(0, 16, masks, 0)
    lax.fori_loop(0, 16, columns, 0)
    dense(0, 6)
    pl.semaphore_wait(barrier, len(partners))

    offset = [0]

    def more(lo, hi):
        offset[0] = near_green(lo, hi, offset[0])

    spread = [copy(D0, RA.at[d - 1], 0, other_z(d)) for d in range(1, 16)]
    begin(spread)
    edge_points = rim(PR, 1)
    begin(edge_points)
    dense(6, 16)
    finish(edge_points)
    more(0, 4)
    all_of(RA, 0, other_z(1))
    total = D0[...]
    for d in range(15):
        total = total + RA[d]
    weight = qw[...] * (SIDE**3 / 128)
    CV[1] = weight * total

    def moments(values, cells):
        tiles = []
        for c in range(16):
            one = slice(c, c + 1)
            z = select_rows(row8 % 4, [LG[2, d, one, :] for d in range(4)])
            parts = [v[one, :] for v in values]
            tiles.append(z * jnp.where(row8 < 4, parts[0], parts[1] if len(parts) > 1 else 0.0))
        for half in range(2):
            rows = jnp.concatenate(tiles[half * 8 : half * 8 + 8], axis=0)
            every = lax.dot_general(rows, A[half], LANES, precision=HI, preferred_element_type=F32)
            total = jnp.zeros((8, 128), F32)
            for c in range(8):
                total = jnp.where(lane // 16 == c, every[c * 8 : c * 8 + 8], total)
            cells[1, half] = total
        wide = jnp.concatenate(tiles, axis=1)
        return lax.dot_general(wide, AP[...], LANES, precision=HI, preferred_element_type=F32)

    def send_planes(small, own, got, i):
        own[...] = jnp.zeros((8, 128), F32)
        own[:, 0:16] = small
        got[0] = own[...]
        begin([copy(own, got.at[d], i, other_g(d)) for d in range(1, 32)])

    def take_planes(got, i, count):
        all_of(got.at[1:32], i, other_g(1))
        low = got[0:16].reshape(128, 128).T[0:16]
        high = got[16:32].reshape(128, 128).T[0:16]
        first = lane // 4 % 2 == 0
        parts = [jnp.where(first, low, pltpu.roll(high, 4, 1))]
        if count == 2:
            parts.append(jnp.where(first, pltpu.roll(low, 124, 1), high))
        for v, part in enumerate(parts):
            ZF[v] = jnp.where(jnp.abs(level_of - g) >= 2, part, 0.0)

    edge_charge = rim(CV, 3)
    begin(edge_charge)
    small = moments([CV.at[1]], MC)
    edge_moments = rim(MC, 5)
    begin(edge_moments)
    send_planes(small, QC, RC, 7)
    more(4, 6)
    finish(edge_charge)
    finish(edge_moments)

    acc = jnp.zeros((128, 128), F32)

    def near_hartree(p, acc):
        for i in range(3):
            slot = near_slot(o, 3 * p + i)
            acc = acc + lax.rsqrt(near_r2(o, slot)) * CV[slot // 16, pl.ds(slot % 16, 1), :]
        return acc

    acc = lax.fori_loop(0, near_count(o) // 3, near_hartree, acc)
    far_xy(o)

    def far_hartree(lev, acc):
        for half in range(2):
            mask = FM[o, pl.ds(lev * 2 + half, 1), :]
            for d in range(4):
                row = MC[lev, half, d : d + 1, :] * mask
                acc = acc + lax.rsqrt(DXY[half] + far_dz2(o, lev, d)) * row
        return acc

    acc = lax.fori_loop(0, 3, far_hartree, acc)
    plane_z(o)
    more(6, 7)
    take_planes(RC, 7, 1)

    def plane_hartree(a, acc):
        xz2 = plane_xz2(o, a)
        for b in range(4):
            acc = acc + lax.rsqrt(xz2 + DXY[1 + b]) * ZF[0, pl.ds(a * 4 + b, 1), :]
        return acc

    acc = lax.fori_loop(0, 4, plane_hartree, acc)
    HG[0] = jnp.sum(acc.T, axis=0, keepdims=True)
    begin([copy(HG.at[0], HG.at[d], 8, other_z(d)) for d in range(1, 16)])
    more(7, 14)
    all_of(HG.at[1:16], 8, other_z(1))
    for d in range(16):
        hart[pl.ds((o + 16 - d) % 16, 1), :] = HG[d]

    scaled = weight * (ext[...] + hart[...])
    for v in range(2):
        SV[1, v] = scaled * orb[v]
    edge_sources = rim(SV, 9)
    begin(edge_sources)
    small = moments([SV.at[1, 0], SV.at[1, 1]], MS)
    edge_moments = rim(MS, 11)
    begin(edge_moments)
    send_planes(small, QS, RS, 13)
    more(14, 16)

    def weigh(values, rows):
        total = None
        for value, row in zip(values, rows):
            term = value.astype(F32) * row
            total = term if total is None else total + term
        return total

    def local(lo, hi, off):
        def cell(t, off):
            def far(lev, acc):
                acc = list(acc)
                masks = [FM[t, pl.ds(lev * 2 + half, 1), :] for half in range(2)]
                for d in range(4):
                    for v in range(2):
                        r = v * 4 + d
                        at = t * FAR + lev * 8 + d * 2
                        acc[v] = acc[v] + weigh(
                            [G[at, v], G[at + 1, v]],
                            [MS[lev, half, r : r + 1, :] * masks[half] for half in range(2)],
                        )
                return tuple(acc)

            acc = lax.fori_loop(0, 3, far, (jnp.zeros((128, 128), F32),) * 2)
            for v in range(2):
                ACC[t, v] = acc[v]
            count = (near_count(t) + 5) // 6

            def six(p, c):
                slots = [near_slot(t, 6 * p + i) for i in range(6)]
                for v in range(2):
                    total = ACC[t, v]
                    for i, slot in enumerate(slots):
                        row = SV[slot // 16, v, pl.ds(slot % 16, 1), :]
                        total = total + GN[off + p, v, i].astype(F32) * row
                    ACC[t, v] = total
                return c

            lax.fori_loop(0, count, six, 0)
            return off + count

        return lax.fori_loop(lo, hi, cell, off)

    done = [0]

    def apply(lo, hi):
        done[0] = local(lo, hi, done[0])

    finish(edge_sources)
    finish(edge_moments)
    apply(0, 16)
    take_planes(RS, 13, 2)

    def update(t, carry):
        plane_z(t)

        def planes(j, c):
            total = [ACC[t, v] for v in range(2)]
            for a in (2 * j, 2 * j + 1):
                xz2 = plane_xz2(t, a)
                for b in range(4):
                    r2 = xz2 + DXY[1 + b]
                    inv = lax.rsqrt(r2)
                    s = r2 * inv
                    for v in range(2):
                        row = ZF[v, pl.ds(a * 4 + b, 1), :]
                        total[v] = total[v] + jnp.exp2(s * rates[v]) * (inv * row)
            for v in range(2):
                ACC[t, v] = total[v]
            return c

        lax.fori_loop(0, 2, planes, 0)
        for v in range(2):
            out[v, pl.ds(t, 1), :] = SCALE * jnp.sum(ACC[t, v].T, axis=0, keepdims=True)
        return carry

    lax.fori_loop(0, 16, update, 0)


def body(orbitals, points, quad_weight, external, screening, level_index, near_cells, far_cells):
    vmem = pl.BlockSpec(memory_space=pltpu.VMEM)
    smem = pl.BlockSpec(memory_space=pltpu.SMEM)

    def f32(*shape):
        return pltpu.VMEM(shape, F32)

    def bf16(*shape):
        return pltpu.VMEM(shape, BF16)

    return pl.pallas_call(
        kernel,
        out_shape=(
            jax.ShapeDtypeStruct((2, 16, 128), F32),
            jax.ShapeDtypeStruct((16, 128), F32),
        ),
        in_specs=[vmem] * 4 + [smem] * 3,
        out_specs=(vmem, vmem),
        scratch_shapes=[
            bf16(16 * FAR, 2, 128, 128),
            bf16(NEAR, 2, 6, 128, 128),
            f32(16, 2, 128, 128),
            f32(16, 3, 128, 128),
            f32(5, 128, 128),
            f32(4, 3, 16, 128),
            f32(4, 16, 128),
            f32(4, 2, 16, 128),
            f32(3, 2, 8, 128),
            f32(3, 2, 8, 128),
            f32(3, 4, 16, 128),
            f32(2, 4, 16, 128),
            f32(2, 128, 128),
            f32(16, 2048),
            f32(16, 128),
            f32(15, 16, 128),
            f32(8, 128),
            f32(32, 8, 128),
            f32(8, 128),
            f32(32, 8, 128),
            f32(2, 16, 128),
            f32(16, 1, 128),
            f32(16, 8, 128),
            pltpu.SemaphoreType.DMA((14,)),
            pltpu.SemaphoreType.DMA((14,)),
        ],
        compiler_params=pltpu.CompilerParams(
            collective_id=0, has_side_effects=True, vmem_limit_bytes=67043328
        ),
        name="green_step",
    )(orbitals, points, quad_weight, external, screening, level_index, near_cells)


def solution(mesh):
    in_specs = (
        P("orb", "space", None),
        P(None, "space", None),
        P("space", None),
        P("space", None),
        P(),
        P("orb"),
        P("space", None),
        P("space", None),
    )
    out_specs = (P("orb", "space", None), P("space", None))
    return jax.shard_map(body, mesh=mesh, in_specs=in_specs, out_specs=out_specs, check_vma=False)
```

```python
import functools
import math

import jax
import jax.numpy as jnp
from jax import lax
from jax.experimental import pallas as pl
from jax.experimental.pallas import tpu as pltpu
from jax.sharding import PartitionSpec as P

F32 = jnp.float32
BF16 = jnp.bfloat16
HI = lax.Precision.HIGHEST
LANES = (((1,), (1,)), ((), ()))
SOFTEN = 6.25e-06
SCALE = -0.5 / math.pi
SIDE = 0.25
NODE = [math.cos((2 * a + 1) * math.pi / 8) for a in range(4)]
OFFSET = [0.5 * (t + 1.0) for t in NODE]
FAR = 12
PLANE = 8
DENSE = FAR + PLANE
NEAR = 4 * 2 + 8 * 3 + 4 * 5

CORNERS = (0, 3, 12, 15)
EDGES = (1, 2, 4, 7, 8, 11, 13, 14)
INNER = (5, 6, 9, 10)
SIXES = [2 if t in CORNERS else 5 if t in INNER else 3 for t in range(16)]
FIRST = [sum(SIXES[:t]) for t in range(16)]


def iota(shape, axis):
    return lax.broadcasted_iota(jnp.int32, shape, axis)


def pick(index, table):
    out = jnp.full(index.shape, table[0], F32)
    for i in range(1, 4):
        out = jnp.where(index == i, F32(table[i]), out)
    return out


def pick_scalar(index, table):
    out = F32(table[0])
    for i in range(1, 4):
        out = jnp.where(index == i, F32(table[i]), out)
    return out


def pick_int(index, table):
    out = jnp.int32(table[0])
    for i in range(1, len(table)):
        out = jnp.where(index == i, jnp.int32(table[i]), out)
    return out


def select_rows(row, parts):
    out = jnp.where(row == 0, parts[0], parts[1])
    for i in range(2, 4):
        out = jnp.where(row == i, parts[i], out)
    return out


def hi_lo(row):
    r = iota((16, row.shape[1]), 0)
    rest = row - row.astype(BF16).astype(F32)
    return jnp.where(r == 0, row, jnp.where(r == 1, rest, 0.0)).astype(BF16)


def lagrange(u):
    out = []
    for a in range(4):
        term = None
        for n in range(4):
            if n != a:
                factor = (u - NODE[n]) * (1.0 / (NODE[a] - NODE[n]))
                term = factor if term is None else term * factor
        out.append(term)
    return out


def near_count(t):
    cx, cy = t % 4, t // 4
    nx = jnp.where((cx == 0) | (cx == 3), 2, 3)
    ny = jnp.where((cy == 0) | (cy == 3), 2, 3)
    return 3 * nx * ny


def kernel(
    orb, pts, qw, ext, screening, level, near, out, hart,
    G, GN, TB, DXY, GC, DS, FR, VF, VP, PR, CV, SV, MC, MS, LG, LP, A, AP, D0, RA,
    QC, RC, QS, RS, ZF, HG, FM, send, recv,
):
    o = lax.axis_index("orb")
    g = lax.axis_index("space")
    up, down = (g + 1) % 32, (g + 31) % 32
    lane = iota((1, 128), 1)
    away = lane // 8 + 16 * (lane // 4 % 2)
    level_of = (g + 32 - away) % 32

    def other_z(d):
        return {"orb": (o + d) % 16}

    def other_g(d):
        return {"space": (g + d) % 32}

    barrier = pltpu.get_barrier_semaphore()
    partners = [other_z(d) for d in range(1, 16)]
    partners += [other_g(d) for d in range(1, 32)]
    for partner in partners:
        pl.semaphore_signal(barrier, inc=1, device_id=partner, device_id_type=pl.DeviceIdType.MESH)

    def copy(src, dst, i, device):
        return pltpu.make_async_remote_copy(
            src, dst, send.at[i], recv.at[i],
            device_id=device, device_id_type=pl.DeviceIdType.MESH,
        )

    def all_of(ref, i, device):
        whole = copy(ref, ref, i, device)
        whole.wait_send()
        whole.wait_recv()

    def rim(ref, i):
        return [
            copy(ref.at[1], ref.at[0], i, {"space": up}),
            copy(ref.at[1], ref.at[2], i + 1, {"space": down}),
        ]

    def begin(copies):
        for c in copies:
            c.start()

    def finish(copies):
        for c in copies:
            c.wait()

    rates = [-screening[level[v]] * (1.0 / math.log(2.0)) for v in range(2)]

    def columns(t):
        for k in range(3):
            TB[k] = jnp.broadcast_to(pts[k, pl.ds(t, 1), :], (128, 128)).T

    def green(r2):
        inv = lax.rsqrt(r2)
        s = r2 * inv
        return [(jnp.exp2(s * rate) * inv).astype(BF16) for rate in rates]

    def far_xy():
        a, b, c8 = lane // 4 % 4, lane % 4, lane // 16
        gx = (c8 % 4).astype(F32) * SIDE + SIDE * pick(a, OFFSET)
        dx = TB[0] - gx
        for half in range(2):
            gy = (c8 // 4 + 2 * half).astype(F32) * SIDE + SIDE * pick(b, OFFSET)
            dy = TB[1] - gy
            DXY[half] = dx * dx + (dy * dy + SOFTEN)

    def plane_z():
        gz = level_of.astype(F32) * SIDE + SIDE * pick(lane % 4, OFFSET)
        dz = TB[2] - gz
        DXY[0] = dz * dz + SOFTEN
        for b in range(4):
            dy = TB[1] - OFFSET[b]
            DXY[1 + b] = dy * dy

    def far_dz2(lev, d):
        dz = TB[2] - ((g - 1 + lev).astype(F32) * SIDE + SIDE * OFFSET[d])
        return dz * dz

    def plane_xz2(a):
        dx = TB[0] - pick_scalar(a, OFFSET)
        return dx * dx + DXY[0]

    def store_green(block, half, r2):
        for v, values in enumerate(green(r2)):
            G[block, v, half * 128 : half * 128 + 128, :] = values

    def proxy_columns():
        r = iota((128, 128), 0)
        a, b, c8 = r // 4 % 4, r % 4, r // 16
        GC[0] = (c8 % 4).astype(F32) * SIDE + SIDE * pick(a, OFFSET)
        for half in range(2):
            GC[1 + half] = (c8 // 4 + 2 * half).astype(F32) * SIDE + SIDE * pick(b, OFFSET)
        plane = (g + 32 - (r // 8 + 16 * (r // 4 % 2))) % 32
        GC[3] = plane.astype(F32) * SIDE + SIDE * pick(r % 4, OFFSET)

    def dense(lo, hi):
        def cell(t, carry):
            tx, ty, tz = (pts[k, pl.ds(t, 1), :] for k in range(3))
            dx = tx - GC[0]
            dx2 = dx * dx + SOFTEN
            for half in range(2):
                dy = ty - GC[1 + half]
                DS[half] = dx2 + dy * dy
            dz = tz - GC[3]
            DS[2] = dz * dz + SOFTEN

            def far(lev, c):
                for d in range(4):
                    dz = tz - ((g - 1 + lev).astype(F32) * SIDE + SIDE * OFFSET[d])
                    for half in range(2):
                        store_green(t * DENSE + lev * 4 + d, half, DS[half] + dz * dz)
                return c

            lax.fori_loop(0, 3, far, 0)

            def planes(j, c):
                for i in range(2):
                    dx = tx - pick_scalar(2 * j + i, OFFSET)
                    for b in range(4):
                        dy = ty - OFFSET[b]
                        at = t * DENSE + FAR + j * 4 + i * 2 + b // 2
                        store_green(at, b % 2, DS[2] + (dx * dx + dy * dy))
                return c

            lax.fori_loop(0, 2, planes, 0)
            return carry

        lax.fori_loop(lo, hi, cell, 0)

    def near_slot(t, n):
        cell = near[t, jnp.minimum(n, 26)]
        live = (cell >= 0) & (n < 27)
        return jnp.where(live, jnp.clip(cell - 16 * (g - 1), 0, 47), 48)

    def near_r2(slot):
        lev, c = slot // 16, slot % 16
        total = None
        for k in range(3):
            d = TB[k] - PR[lev, k, pl.ds(c, 1), :]
            total = d * d + SOFTEN if total is None else total + d * d
        return total

    def near_green(lo, hi, off):
        def cell(t, off):
            columns(t)
            count = (near_count(t) + 5) // 6

            def six(p, c):
                for i in range(6):
                    for v, values in enumerate(green(near_r2(near_slot(t, 6 * p + i)))):
                        GN[off + p, v, i] = values
                return c

            lax.fori_loop(0, count, six, 0)
            return off + count

        return lax.fori_loop(lo, hi, cell, off)

    D0[...] = 2.0 * (orb[0] * orb[0] + orb[1] * orb[1])
    PR[1] = pts[...]
    PR[3] = jnp.zeros((3, 16, 128), F32)
    CV[3] = jnp.zeros((16, 128), F32)
    SV[3] = jnp.zeros((2, 16, 128), F32)
    row16 = iota((16, 128), 0)
    ux = (pts[0] - (row16 % 4).astype(F32) * SIDE) * (2.0 / SIDE) - 1.0
    uy = (pts[1] - (row16 // 4).astype(F32) * SIDE) * (2.0 / SIDE) - 1.0
    uz = (pts[2] - g.astype(F32) * SIDE) * (2.0 / SIDE) - 1.0
    for k, u in enumerate((ux, uy, uz)):
        for a, w in enumerate(lagrange(u)):
            LG[k, a] = w
    for k in range(2):
        for a, w in enumerate(lagrange(2.0 * pts[k] - 1.0)):
            LP[k, a] = w
    row8 = iota((8, 128), 0)
    for c in range(16):
        one = slice(c, c + 1)
        ycell = select_rows(row8 % 4, [LG[1, b, one, :] for b in range(4)])
        yplane = select_rows(row8 % 4, [LP[1, b, one, :] for b in range(4)])
        for k in range(2):
            xcell = jnp.where(row8 < 4, LG[0, 2 * k, one, :], LG[0, 2 * k + 1, one, :])
            xplane = jnp.where(row8 < 4, LP[0, 2 * k, one, :], LP[0, 2 * k + 1, one, :])
            at = c % 8 * 16 + k * 8
            A[c // 8, at : at + 8, :] = xcell * ycell
            AP[k * 8 : k * 8 + 8, c * 128 : c * 128 + 128] = xplane * yplane

    def masks(t, carry):
        lev = g - 1 + row8 // 2
        cell = lev * 16 + row8 % 2 * 8 + lane // 16
        hit = (lev < 0) | (lev > 31)
        for n in range(27):
            hit = hit | (cell == near[t, n])
        FM[t] = jnp.where(hit, 0.0, 1.0)
        return carry

    lax.fori_loop(0, 16, masks, 0)
    proxy_columns()
    dense(0, 4)
    pl.semaphore_wait(barrier, len(partners))

    offset = [0]

    def more(lo, hi):
        offset[0] = near_green(lo, hi, offset[0])

    spread = [copy(D0, RA.at[d - 1], 0, other_z(d)) for d in range(1, 16)]
    begin(spread)
    edge_points = rim(PR, 1)
    begin(edge_points)
    dense(4, 12)
    finish(edge_points)
    more(0, 3)
    all_of(RA, 0, other_z(1))
    total = D0[...]
    for d in range(15):
        total = total + RA[d]
    weight = qw[...] * (SIDE**3 / 128)
    CV[1] = weight * total

    def moments(values, cells):
        tiles = []
        for c in range(16):
            one = slice(c, c + 1)
            z = select_rows(row8 % 4, [LG[2, d, one, :] for d in range(4)])
            parts = [v[one, :] for v in values]
            tiles.append(z * jnp.where(row8 < 4, parts[0], parts[1] if len(parts) > 1 else 0.0))
        for half in range(2):
            rows = jnp.concatenate(tiles[half * 8 : half * 8 + 8], axis=0)
            every = lax.dot_general(rows, A[half], LANES, precision=HI, preferred_element_type=F32)
            total = jnp.zeros((8, 128), F32)
            for c in range(8):
                total = jnp.where(lane // 16 == c, every[c * 8 : c * 8 + 8], total)
            cells[1, half] = total
        wide = jnp.concatenate(tiles, axis=1)
        return lax.dot_general(wide, AP[...], LANES, precision=HI, preferred_element_type=F32)

    def send_planes(small, own, got, i):
        own[...] = jnp.zeros((8, 128), F32)
        own[:, 0:16] = small
        got[0] = own[...]
        begin([copy(own, got.at[d], i, other_g(d)) for d in range(1, 32)])

    def take_planes(got, i, count):
        all_of(got.at[1:32], i, other_g(1))
        low = got[0:16].reshape(128, 128).T[0:16]
        high = got[16:32].reshape(128, 128).T[0:16]
        first = lane // 4 % 2 == 0
        parts = [jnp.where(first, low, pltpu.roll(high, 4, 1))]
        if count == 2:
            parts.append(jnp.where(first, pltpu.roll(low, 124, 1), high))
        for v, part in enumerate(parts):
            ZF[v] = jnp.where(jnp.abs(level_of - g) >= 2, part, 0.0)

    edge_charge = rim(CV, 3)
    begin(edge_charge)
    small = moments([CV.at[1]], MC)
    edge_moments = rim(MC, 5)
    begin(edge_moments)
    send_planes(small, QC, RC, 7)
    dense(12, 14)
    more(3, 4)
    finish(edge_charge)
    finish(edge_moments)

    columns(o)
    acc = jnp.zeros((128, 128), F32)

    def near_hartree(p, acc):
        for i in range(3):
            slot = near_slot(o, 3 * p + i)
            acc = acc + lax.rsqrt(near_r2(slot)) * CV[slot // 16, pl.ds(slot % 16, 1), :]
        return acc

    acc = lax.fori_loop(0, near_count(o) // 3, near_hartree, acc)
    far_xy()

    def far_hartree(lev, acc):
        for half in range(2):
            mask = FM[o, pl.ds(lev * 2 + half, 1), :]
            for d in range(4):
                row = MC[lev, half, d : d + 1, :] * mask
                acc = acc + lax.rsqrt(DXY[half] + far_dz2(lev, d)) * row
        return acc

    acc = lax.fori_loop(0, 3, far_hartree, acc)
    plane_z()
    take_planes(RC, 7, 1)

    def plane_hartree(a, acc):
        xz2 = plane_xz2(a)
        for b in range(4):
            acc = acc + lax.rsqrt(xz2 + DXY[1 + b]) * ZF[0, pl.ds(a * 4 + b, 1), :]
        return acc

    acc = lax.fori_loop(0, 4, plane_hartree, acc)
    HG[0] = jnp.sum(acc.T, axis=0, keepdims=True)
    begin([copy(HG.at[0], HG.at[d], 8, other_z(d)) for d in range(1, 16)])
    more(4, 12)
    all_of(HG.at[1:16], 8, other_z(1))
    for d in range(16):
        hart[pl.ds((o + 16 - d) % 16, 1), :] = HG[d]

    scaled = weight * (ext[...] + hart[...])
    for v in range(2):
        SV[1, v] = scaled * orb[v]
    edge_sources = rim(SV, 9)
    begin(edge_sources)
    small = moments([SV.at[1, 0], SV.at[1, 1]], MS)
    edge_moments = rim(MS, 11)
    begin(edge_moments)
    send_planes(small, QS, RS, 13)
    more(12, 16)
    dense(14, 16)

    finish(edge_sources)
    finish(edge_moments)
    for v in range(2):
        for lev in range(3):
            for d in range(4):
                r = v * 4 + d
                rows = [MS[lev, half, r : r + 1, :] for half in range(2)]
                VF[lev * 4 + d, v] = hi_lo(jnp.concatenate(rows, axis=1))

    def product(rows, block, v):
        return lax.dot_general(
            rows, G[block, v], (((1,), (0,)), ((), ())), preferred_element_type=F32
        )

    def local(cells, sixes):
        def cell(i, carry):
            t = pick_int(i, cells)
            off = pick_int(i, [FIRST[c] for c in cells])
            far = [jnp.zeros((16, 128), F32) for _ in range(2)]
            for lev in range(3):
                mask = jnp.concatenate(
                    [
                        jnp.broadcast_to(FM[t, lev * 2 + half : lev * 2 + half + 1, :], (16, 128))
                        for half in range(2)
                    ],
                    axis=1,
                ).astype(BF16)
                for d in range(4):
                    k = lev * 4 + d
                    for v in range(2):
                        far[v] = far[v] + product(VF[k, v] * mask, t * DENSE + k, v)
            slots = [near_slot(t, n) for n in range(6 * sixes)]
            for v in range(2):
                total = None
                for n, slot in enumerate(slots):
                    row = SV[slot // 16, v, pl.ds(slot % 16, 1), :]
                    term = GN[off + n // 6, v, n % 6].astype(F32) * row
                    total = term if total is None else total + term
                near_row = jnp.sum(total.T, axis=0, keepdims=True)
                FR[v, pl.ds(t, 1), :] = near_row + (far[v][0:1] + far[v][1:2])
            return carry

        lax.fori_loop(0, len(cells), cell, 0)

    local(CORNERS, 2)
    local(EDGES, 3)
    local(INNER, 5)
    take_planes(RS, 13, 2)
    for v in range(2):
        for k in range(PLANE):
            rows = [ZF[v, 2 * k + half : 2 * k + half + 1, :] for half in range(2)]
            VP[k, v] = hi_lo(jnp.concatenate(rows, axis=1))

    def update(t, carry):
        for v in range(2):
            acc = jnp.zeros((16, 128), F32)
            for k in range(PLANE):
                acc = acc + product(VP[k, v], t * DENSE + FAR + k, v)
            row = FR[v, pl.ds(t, 1), :] + (acc[0:1] + acc[1:2])
            out[v, pl.ds(t, 1), :] = SCALE * row
        return carry

    lax.fori_loop(0, 16, update, 0, unroll=2)


def body(orbitals, points, quad_weight, external, screening, level_index, near_cells, far_cells):
    vmem = pl.BlockSpec(memory_space=pltpu.VMEM)
    smem = pl.BlockSpec(memory_space=pltpu.SMEM)

    def f32(*shape):
        return pltpu.VMEM(shape, F32)

    def bf16(*shape):
        return pltpu.VMEM(shape, BF16)

    return pl.pallas_call(
        kernel,
        out_shape=(
            jax.ShapeDtypeStruct((2, 16, 128), F32),
            jax.ShapeDtypeStruct((16, 128), F32),
        ),
        in_specs=[vmem] * 4 + [smem] * 3,
        out_specs=(vmem, vmem),
        scratch_shapes=[
            bf16(16 * DENSE, 2, 256, 128),
            bf16(NEAR, 2, 6, 128, 128),
            f32(3, 128, 128),
            f32(5, 128, 128),
            f32(4, 128, 128),
            f32(3, 128, 128),
            f32(2, 16, 128),
            bf16(FAR, 2, 16, 256),
            bf16(PLANE, 2, 16, 256),
            f32(4, 3, 16, 128),
            f32(4, 16, 128),
            f32(4, 2, 16, 128),
            f32(3, 2, 8, 128),
            f32(3, 2, 8, 128),
            f32(3, 4, 16, 128),
            f32(2, 4, 16, 128),
            f32(2, 128, 128),
            f32(16, 2048),
            f32(16, 128),
            f32(15, 16, 128),
            f32(8, 128),
            f32(32, 8, 128),
            f32(8, 128),
            f32(32, 8, 128),
            f32(2, 16, 128),
            f32(16, 1, 128),
            f32(16, 8, 128),
            pltpu.SemaphoreType.DMA((14,)),
            pltpu.SemaphoreType.DMA((14,)),
        ],
        compiler_params=pltpu.CompilerParams(
            collective_id=0, has_side_effects=True, vmem_limit_bytes=67043328
        ),
        name="green_step",
    )(orbitals, points, quad_weight, external, screening, level_index, near_cells)


def solution(mesh):
    in_specs = (
        P("orb", "space", None),
        P(None, "space", None),
        P("space", None),
        P("space", None),
        P(),
        P("orb"),
        P("space", None),
        P("space", None),
    )
    out_specs = (P("orb", "space", None), P("space", None))
    return jax.shard_map(body, mesh=mesh, in_specs=in_specs, out_specs=out_specs, check_vma=False)
```

```python
import functools
import math

import jax
import jax.numpy as jnp
from jax import lax
from jax.experimental import pallas as pl
from jax.experimental.pallas import tpu as pltpu
from jax.sharding import PartitionSpec as P

F32 = jnp.float32
BF16 = jnp.bfloat16
HI = lax.Precision.HIGHEST
LANES = (((1,), (1,)), ((), ()))
SOFTEN = 6.25e-06
SCALE = -0.5 / math.pi
SIDE = 0.25
NODE = [math.cos((2 * a + 1) * math.pi / 8) for a in range(4)]
OFFSET = [0.5 * (t + 1.0) for t in NODE]
FAR = 12
PLANE = 8
DENSE = FAR + PLANE
NEAR = 4 * 12 + 8 * 18 + 4 * 27

CORNERS = (0, 3, 12, 15)
EDGES = (1, 2, 4, 7, 8, 11, 13, 14)
INNER = (5, 6, 9, 10)
NEAREST = [12 if t in CORNERS else 27 if t in INNER else 18 for t in range(16)]
FIRST = [sum(NEAREST[:t]) for t in range(16)]


def iota(shape, axis):
    return lax.broadcasted_iota(jnp.int32, shape, axis)


def pick(index, table):
    out = jnp.full(index.shape, table[0], F32)
    for i in range(1, 4):
        out = jnp.where(index == i, F32(table[i]), out)
    return out


def pick_scalar(index, table):
    out = F32(table[0])
    for i in range(1, 4):
        out = jnp.where(index == i, F32(table[i]), out)
    return out


def pick_int(index, table):
    out = index * 0 + table[0]
    for i in range(1, len(table)):
        out = jnp.where(index == i, jnp.int32(table[i]), out)
    return out


def select_rows(row, parts):
    out = jnp.where(row == 0, parts[0], parts[1])
    for i in range(2, 4):
        out = jnp.where(row == i, parts[i], out)
    return out


def hi_lo(row):
    r = iota((16, row.shape[1]), 0)
    rest = row - row.astype(BF16).astype(F32)
    return jnp.where(r == 0, row, jnp.where(r == 1, rest, 0.0)).astype(BF16)


def lagrange(u):
    out = []
    for a in range(4):
        term = None
        for n in range(4):
            if n != a:
                factor = (u - NODE[n]) * (1.0 / (NODE[a] - NODE[n]))
                term = factor if term is None else term * factor
        out.append(term)
    return out


def near_count(t):
    cx, cy = t % 4, t // 4
    nx = jnp.where((cx == 0) | (cx == 3), 2, 3)
    ny = jnp.where((cy == 0) | (cy == 3), 2, 3)
    return 3 * nx * ny


def kernel(
    orb, pts, qw, ext, screening, level, near, both,
    G, GN, TB, DXY, GC, DS, FR, VF, VP, PR, CV, SV, MC, MS, LG, LP, A, AP, D0, RA,
    QC, RC, QS, RS, ZF, HG, FM, send, recv,
):
    o = lax.axis_index("orb")
    g = lax.axis_index("space")
    up, down = (g + 1) % 32, (g + 31) % 32
    hart = both.at[2]
    lane = iota((1, 128), 1)
    away = lane // 8 + 16 * (lane // 4 % 2)
    level_of = (g + 32 - away) % 32

    def other_z(d):
        return {"orb": (o + d) % 16}

    def other_g(d):
        return {"space": (g + d) % 32}

    barrier = pltpu.get_barrier_semaphore()
    partners = [other_z(d) for d in range(1, 16)]
    partners += [other_g(d) for d in range(1, 32)]
    for partner in partners:
        pl.semaphore_signal(barrier, inc=1, device_id=partner, device_id_type=pl.DeviceIdType.MESH)

    def copy(src, dst, i, device):
        return pltpu.make_async_remote_copy(
            src, dst, send.at[i], recv.at[i],
            device_id=device, device_id_type=pl.DeviceIdType.MESH,
        )

    def all_of(ref, i, device):
        whole = copy(ref, ref, i, device)
        whole.wait_send()
        whole.wait_recv()

    def rim(ref, i):
        return [
            copy(ref.at[1], ref.at[0], i, {"space": up}),
            copy(ref.at[1], ref.at[2], i + 1, {"space": down}),
        ]

    def begin(copies):
        for c in copies:
            c.start()

    def finish(copies):
        for c in copies:
            c.wait()

    rates = [-screening[level[v]] * (1.0 / math.log(2.0)) for v in range(2)]

    def columns(t):
        for k in range(3):
            TB[k] = jnp.broadcast_to(pts[k, pl.ds(t, 1), :], (128, 128)).T

    def green(r2):
        inv = lax.rsqrt(r2)
        s = r2 * inv
        return [(jnp.exp2(s * rate) * inv).astype(BF16) for rate in rates]

    def far_xy():
        a, b, c8 = lane // 4 % 4, lane % 4, lane // 16
        gx = (c8 % 4).astype(F32) * SIDE + SIDE * pick(a, OFFSET)
        dx = TB[0] - gx
        for half in range(2):
            gy = (c8 // 4 + 2 * half).astype(F32) * SIDE + SIDE * pick(b, OFFSET)
            dy = TB[1] - gy
            DXY[half] = dx * dx + (dy * dy + SOFTEN)

    def plane_z():
        gz = level_of.astype(F32) * SIDE + SIDE * pick(lane % 4, OFFSET)
        dz = TB[2] - gz
        DXY[0] = dz * dz + SOFTEN
        for b in range(4):
            dy = TB[1] - OFFSET[b]
            DXY[1 + b] = dy * dy

    def far_dz2(lev, d):
        dz = TB[2] - ((g - 1 + lev).astype(F32) * SIDE + SIDE * OFFSET[d])
        return dz * dz

    def plane_xz2(a):
        dx = TB[0] - pick_scalar(a, OFFSET)
        return dx * dx + DXY[0]

    def store_green(block, half, r2):
        for v, values in enumerate(green(r2)):
            G[block, v, half * 128 : half * 128 + 128, :] = values

    def proxy_columns():
        r = iota((128, 128), 0)
        a, b, c8 = r // 4 % 4, r % 4, r // 16
        GC[0] = (c8 % 4).astype(F32) * SIDE + SIDE * pick(a, OFFSET)
        for half in range(2):
            GC[1 + half] = (c8 // 4 + 2 * half).astype(F32) * SIDE + SIDE * pick(b, OFFSET)
        plane = (g + 32 - (r // 8 + 16 * (r // 4 % 2))) % 32
        GC[3] = plane.astype(F32) * SIDE + SIDE * pick(r % 4, OFFSET)

    def dense(lo, hi):
        def cell(t, carry):
            tx, ty, tz = (pts[k, pl.ds(t, 1), :] for k in range(3))
            dx = tx - GC[0]
            dx2 = dx * dx + SOFTEN
            for half in range(2):
                dy = ty - GC[1 + half]
                DS[half] = dx2 + dy * dy
            dz = tz - GC[3]
            DS[2] = dz * dz + SOFTEN

            def far(lev, c):
                for d in range(4):
                    dz = tz - ((g - 1 + lev).astype(F32) * SIDE + SIDE * OFFSET[d])
                    for half in range(2):
                        store_green(t * DENSE + lev * 4 + d, half, DS[half] + dz * dz)
                return c

            lax.fori_loop(0, 3, far, 0)

            def planes(j, c):
                for i in range(2):
                    dx = tx - pick_scalar(2 * j + i, OFFSET)
                    for b in range(4):
                        dy = ty - OFFSET[b]
                        at = t * DENSE + FAR + j * 4 + i * 2 + b // 2
                        store_green(at, b % 2, DS[2] + (dx * dx + dy * dy))
                return c

            lax.fori_loop(0, 2, planes, 0)
            return carry

        lax.fori_loop(lo, hi, cell, 0)

    def near_slot(t, n):
        cell = near[t, n]
        return jnp.where(cell >= 0, jnp.clip(cell - 16 * (g - 1), 0, 47), 48)

    def near_r2(slot):
        lev, c = slot // 16, slot % 16
        total = None
        for k in range(3):
            d = TB[k] - PR[lev, k, pl.ds(c, 1), :]
            total = d * d + SOFTEN if total is None else total + d * d
        return total

    def near_green(cells):
        count = NEAREST[cells[0]]

        def cell(i, carry):
            t = pick_int(i, cells)
            off = pick_int(i, [FIRST[c] for c in cells])
            columns(t)
            for n in range(count):
                for v, values in enumerate(green(near_r2(near_slot(t, n)))):
                    GN[off + n, v] = values
            return carry

        lax.fori_loop(0, len(cells), cell, 0)

    D0[...] = 2.0 * (orb[0] * orb[0] + orb[1] * orb[1])
    PR[1] = pts[...]
    PR[3] = jnp.zeros((3, 16, 128), F32)
    CV[3] = jnp.zeros((16, 128), F32)
    SV[3] = jnp.zeros((2, 16, 128), F32)
    row16 = iota((16, 128), 0)
    ux = (pts[0] - (row16 % 4).astype(F32) * SIDE) * (2.0 / SIDE) - 1.0
    uy = (pts[1] - (row16 // 4).astype(F32) * SIDE) * (2.0 / SIDE) - 1.0
    uz = (pts[2] - g.astype(F32) * SIDE) * (2.0 / SIDE) - 1.0
    for k, u in enumerate((ux, uy, uz)):
        for a, w in enumerate(lagrange(u)):
            LG[k, a] = w
    for k in range(2):
        for a, w in enumerate(lagrange(2.0 * pts[k] - 1.0)):
            LP[k, a] = w
    row8 = iota((8, 128), 0)
    for c in range(16):
        one = slice(c, c + 1)
        ycell = select_rows(row8 % 4, [LG[1, b, one, :] for b in range(4)])
        yplane = select_rows(row8 % 4, [LP[1, b, one, :] for b in range(4)])
        for k in range(2):
            xcell = jnp.where(row8 < 4, LG[0, 2 * k, one, :], LG[0, 2 * k + 1, one, :])
            xplane = jnp.where(row8 < 4, LP[0, 2 * k, one, :], LP[0, 2 * k + 1, one, :])
            at = c % 8 * 16 + k * 8
            A[c // 8, at : at + 8, :] = xcell * ycell
            AP[k * 8 : k * 8 + 8, c * 128 : c * 128 + 128] = xplane * yplane

    def masks(t, carry):
        lev = g - 1 + row8 // 2
        cell = lev * 16 + row8 % 2 * 8 + lane // 16
        hit = (lev < 0) | (lev > 31)
        for n in range(27):
            hit = hit | (cell == near[t, n])
        FM[t] = jnp.where(hit, 0.0, 1.0)
        return carry

    lax.fori_loop(0, 16, masks, 0)
    proxy_columns()
    dense(0, 4)
    pl.semaphore_wait(barrier, len(partners))

    spread = [copy(D0, RA.at[d - 1], 0, other_z(d)) for d in range(1, 16)]
    begin(spread)
    edge_points = rim(PR, 1)
    begin(edge_points)
    dense(4, 12)
    finish(edge_points)
    near_green(CORNERS)
    all_of(RA, 0, other_z(1))
    total = D0[...]
    for d in range(15):
        total = total + RA[d]
    weight = qw[...] * (SIDE**3 / 128)
    CV[1] = weight * total

    def moments(values, cells):
        tiles = []
        for c in range(16):
            one = slice(c, c + 1)
            z = select_rows(row8 % 4, [LG[2, d, one, :] for d in range(4)])
            parts = [v[one, :] for v in values]
            tiles.append(z * jnp.where(row8 < 4, parts[0], parts[1] if len(parts) > 1 else 0.0))
        for half in range(2):
            rows = jnp.concatenate(tiles[half * 8 : half * 8 + 8], axis=0)
            every = lax.dot_general(rows, A[half], LANES, precision=HI, preferred_element_type=F32)
            total = jnp.zeros((8, 128), F32)
            for c in range(8):
                total = jnp.where(lane // 16 == c, every[c * 8 : c * 8 + 8], total)
            cells[1, half] = total
        wide = jnp.concatenate(tiles, axis=1)
        return lax.dot_general(wide, AP[...], LANES, precision=HI, preferred_element_type=F32)

    def send_planes(small, own, got, i):
        own[...] = jnp.zeros((8, 128), F32)
        own[:, 0:16] = small
        got[0] = own[...]
        begin([copy(own, got.at[d], i, other_g(d)) for d in range(1, 32)])

    def take_planes(got, i, count):
        all_of(got.at[1:32], i, other_g(1))
        low = got[0:16].reshape(128, 128).T[0:16]
        high = got[16:32].reshape(128, 128).T[0:16]
        first = lane // 4 % 2 == 0
        parts = [jnp.where(first, low, pltpu.roll(high, 4, 1))]
        if count == 2:
            parts.append(jnp.where(first, pltpu.roll(low, 124, 1), high))
        for v, part in enumerate(parts):
            ZF[v] = jnp.where(jnp.abs(level_of - g) >= 2, part, 0.0)

    edge_charge = rim(CV, 3)
    begin(edge_charge)
    small = moments([CV.at[1]], MC)
    edge_moments = rim(MC, 5)
    begin(edge_moments)
    send_planes(small, QC, RC, 7)
    dense(12, 14)
    near_green(INNER[:1])
    finish(edge_charge)
    finish(edge_moments)

    columns(o)
    acc = jnp.zeros((128, 128), F32)

    def near_hartree(p, acc):
        for i in range(3):
            slot = near_slot(o, 3 * p + i)
            acc = acc + lax.rsqrt(near_r2(slot)) * CV[slot // 16, pl.ds(slot % 16, 1), :]
        return acc

    acc = lax.fori_loop(0, near_count(o) // 3, near_hartree, acc)
    far_xy()

    def far_hartree(lev, acc):
        for half in range(2):
            mask = FM[o, pl.ds(lev * 2 + half, 1), :]
            for d in range(4):
                row = MC[lev, half, d : d + 1, :] * mask
                acc = acc + lax.rsqrt(DXY[half] + far_dz2(lev, d)) * row
        return acc

    acc = lax.fori_loop(0, 3, far_hartree, acc)
    plane_z()
    take_planes(RC, 7, 1)

    def plane_hartree(a, acc):
        xz2 = plane_xz2(a)
        for b in range(4):
            acc = acc + lax.rsqrt(xz2 + DXY[1 + b]) * ZF[0, pl.ds(a * 4 + b, 1), :]
        return acc

    acc = lax.fori_loop(0, 4, plane_hartree, acc)
    HG[0] = jnp.sum(acc.T, axis=0, keepdims=True)
    begin([copy(HG.at[0], HG.at[d], 8, other_z(d)) for d in range(1, 16)])
    near_green(EDGES)
    dense(14, 15)
    all_of(HG.at[1:16], 8, other_z(1))
    for d in range(16):
        hart[pl.ds((o + 16 - d) % 16, 1), :] = HG[d]

    scaled = weight * (ext[...] + hart[...])
    for v in range(2):
        SV[1, v] = scaled * orb[v]
    edge_sources = rim(SV, 9)
    begin(edge_sources)
    small = moments([SV.at[1, 0], SV.at[1, 1]], MS)
    edge_moments = rim(MS, 11)
    begin(edge_moments)
    send_planes(small, QS, RS, 13)
    near_green(INNER[1:])
    dense(15, 16)

    finish(edge_sources)
    finish(edge_moments)
    for v in range(2):
        for lev in range(3):
            for d in range(4):
                r = v * 4 + d
                rows = [MS[lev, half, r : r + 1, :] for half in range(2)]
                VF[lev * 4 + d, v] = hi_lo(jnp.concatenate(rows, axis=1))

    def product(rows, block, v):
        return lax.dot_general(
            rows, G[block, v], (((1,), (0,)), ((), ())), preferred_element_type=F32
        )

    def local(cells):
        def cell(i, carry):
            t = pick_int(i, cells)
            off = pick_int(i, [FIRST[c] for c in cells])
            far = [jnp.zeros((16, 128), F32) for _ in range(2)]
            for lev in range(3):
                mask = jnp.concatenate(
                    [
                        jnp.broadcast_to(FM[t, lev * 2 + half : lev * 2 + half + 1, :], (16, 128))
                        for half in range(2)
                    ],
                    axis=1,
                ).astype(BF16)
                for d in range(4):
                    k = lev * 4 + d
                    for v in range(2):
                        far[v] = far[v] + product(VF[k, v] * mask, t * DENSE + k, v)
            slots = [near_slot(t, n) for n in range(NEAREST[cells[0]])]
            for v in range(2):
                total = None
                for n, slot in enumerate(slots):
                    row = SV[slot // 16, v, pl.ds(slot % 16, 1), :]
                    term = GN[off + n, v].astype(F32) * row
                    total = term if total is None else total + term
                near_row = jnp.sum(total.T, axis=0, keepdims=True)
                FR[v, pl.ds(t, 1), :] = near_row + (far[v][0:1] + far[v][1:2])
            return carry

        lax.fori_loop(0, len(cells), cell, 0, unroll=2)

    local(CORNERS)
    local(EDGES)
    local(INNER)
    take_planes(RS, 13, 2)
    for v in range(2):
        for k in range(PLANE):
            rows = [ZF[v, 2 * k + half : 2 * k + half + 1, :] for half in range(2)]
            VP[k, v] = hi_lo(jnp.concatenate(rows, axis=1))

    def update(t, carry):
        for v in range(2):
            acc = jnp.zeros((16, 128), F32)
            for k in range(PLANE):
                acc = acc + product(VP[k, v], t * DENSE + FAR + k, v)
            row = FR[v, pl.ds(t, 1), :] + (acc[0:1] + acc[1:2])
            both[v, pl.ds(t, 1), :] = SCALE * row
        return carry

    lax.fori_loop(0, 16, update, 0, unroll=2)


def body(orbitals, points, quad_weight, external, screening, level_index, near_cells, far_cells):
    vmem = pl.BlockSpec(memory_space=pltpu.VMEM)
    smem = pl.BlockSpec(memory_space=pltpu.SMEM)

    def f32(*shape):
        return pltpu.VMEM(shape, F32)

    def bf16(*shape):
        return pltpu.VMEM(shape, BF16)

    both = pl.pallas_call(
        kernel,
        out_shape=jax.ShapeDtypeStruct((3, 16, 128), F32),
        in_specs=[vmem] * 4 + [smem] * 3,
        out_specs=vmem,
        scratch_shapes=[
            bf16(16 * DENSE, 2, 256, 128),
            bf16(NEAR, 2, 128, 128),
            f32(3, 128, 128),
            f32(5, 128, 128),
            f32(4, 128, 128),
            f32(3, 128, 128),
            f32(2, 16, 128),
            bf16(FAR, 2, 16, 256),
            bf16(PLANE, 2, 16, 256),
            f32(4, 3, 16, 128),
            f32(4, 16, 128),
            f32(4, 2, 16, 128),
            f32(3, 2, 8, 128),
            f32(3, 2, 8, 128),
            f32(3, 4, 16, 128),
            f32(2, 4, 16, 128),
            f32(2, 128, 128),
            f32(16, 2048),
            f32(16, 128),
            f32(15, 16, 128),
            f32(8, 128),
            f32(32, 8, 128),
            f32(8, 128),
            f32(32, 8, 128),
            f32(2, 16, 128),
            f32(16, 1, 128),
            f32(16, 8, 128),
            pltpu.SemaphoreType.DMA((14,)),
            pltpu.SemaphoreType.DMA((14,)),
        ],
        compiler_params=pltpu.CompilerParams(
            collective_id=0, has_side_effects=True, vmem_limit_bytes=67043328
        ),
        name="green_step",
    )(orbitals, points, quad_weight, external, screening, level_index, near_cells)
    return both[:2], both[2]


def solution(mesh):
    in_specs = (
        P("orb", "space", None),
        P(None, "space", None),
        P("space", None),
        P("space", None),
        P(),
        P("orb"),
        P("space", None),
        P("space", None),
    )
    out_specs = (P("orb", "space", None), P("space", None))
    return jax.shard_map(body, mesh=mesh, in_specs=in_specs, out_specs=out_specs, check_vma=False)
```

```python
import functools
import math

import jax
import jax.numpy as jnp
from jax import lax
from jax.experimental import pallas as pl
from jax.experimental.pallas import tpu as pltpu
from jax.sharding import PartitionSpec as P

F32 = jnp.float32
BF16 = jnp.bfloat16
HI = lax.Precision.HIGHEST
LANES = (((1,), (1,)), ((), ()))
SOFTEN = 6.25e-06
SCALE = -0.5 / math.pi
SIDE = 0.25
NODE = [math.cos((2 * a + 1) * math.pi / 8) for a in range(4)]
OFFSET = [0.5 * (t + 1.0) for t in NODE]
FAR = 12
PLANE = 8
DENSE = FAR + PLANE
NEAR = 4 * 12 + 8 * 18 + 4 * 27

CORNERS = (0, 3, 12, 15)
EDGES = (1, 2, 4, 7, 8, 11, 13, 14)
INNER = (5, 6, 9, 10)
NEAREST = [12 if t in CORNERS else 27 if t in INNER else 18 for t in range(16)]
FIRST = [sum(NEAREST[:t]) for t in range(16)]


def iota(shape, axis):
    return lax.broadcasted_iota(jnp.int32, shape, axis)


def pick(index, table):
    out = jnp.full(index.shape, table[0], F32)
    for i in range(1, 4):
        out = jnp.where(index == i, F32(table[i]), out)
    return out


def pick_scalar(index, table):
    out = F32(table[0])
    for i in range(1, 4):
        out = jnp.where(index == i, F32(table[i]), out)
    return out


def pick_int(index, table):
    out = index * 0 + table[0]
    for i in range(1, len(table)):
        out = jnp.where(index == i, jnp.int32(table[i]), out)
    return out


def select_rows(row, parts):
    out = jnp.where(row == 0, parts[0], parts[1])
    for i in range(2, 4):
        out = jnp.where(row == i, parts[i], out)
    return out


def hi_lo(row):
    r = iota((16, row.shape[1]), 0)
    rest = row - row.astype(BF16).astype(F32)
    return jnp.where(r == 0, row, jnp.where(r == 1, rest, 0.0)).astype(BF16)


def lagrange(u):
    out = []
    for a in range(4):
        term = None
        for n in range(4):
            if n != a:
                factor = (u - NODE[n]) * (1.0 / (NODE[a] - NODE[n]))
                term = factor if term is None else term * factor
        out.append(term)
    return out


def near_count(t):
    cx, cy = t % 4, t // 4
    nx = jnp.where((cx == 0) | (cx == 3), 2, 3)
    ny = jnp.where((cy == 0) | (cy == 3), 2, 3)
    return 3 * nx * ny


def kernel(
    orb, pts, qw, ext, screening, level, near, out, hart,
    G, GN, TB, DXY, GC, DS, FR, VF, VP, PR, CV, SV, MC, MS, LG, LP, A, AP, D0, RA,
    QC, RC, QS, RS, ZF, HG, FM, send, recv,
):
    o = lax.axis_index("orb")
    g = lax.axis_index("space")
    up, down = (g + 1) % 32, (g + 31) % 32
    lane = iota((1, 128), 1)
    away = lane // 8 + 16 * (lane // 4 % 2)
    level_of = (g + 32 - away) % 32

    def other_z(d):
        return {"orb": (o + d) % 16}

    def other_g(d):
        return {"space": (g + d) % 32}

    barrier = pltpu.get_barrier_semaphore()
    partners = [other_z(d) for d in range(1, 16)]
    partners += [other_g(d) for d in range(1, 32)]
    for partner in partners:
        pl.semaphore_signal(barrier, inc=1, device_id=partner, device_id_type=pl.DeviceIdType.MESH)

    def copy(src, dst, i, device):
        return pltpu.make_async_remote_copy(
            src, dst, send.at[i], recv.at[i],
            device_id=device, device_id_type=pl.DeviceIdType.MESH,
        )

    def all_of(ref, i, device):
        whole = copy(ref, ref, i, device)
        whole.wait_send()
        whole.wait_recv()

    def rim(ref, i):
        return [
            copy(ref.at[1], ref.at[0], i, {"space": up}),
            copy(ref.at[1], ref.at[2], i + 1, {"space": down}),
        ]

    def begin(copies):
        for c in copies:
            c.start()

    def finish(copies):
        for c in copies:
            c.wait()

    rates = [-screening[level[v]] * (1.0 / math.log(2.0)) for v in range(2)]

    def columns(t):
        for k in range(3):
            TB[k] = jnp.broadcast_to(pts[k, pl.ds(t, 1), :], (128, 128)).T

    def green(r2):
        inv = lax.rsqrt(r2)
        s = r2 * inv
        return [(jnp.exp2(s * rate) * inv).astype(BF16) for rate in rates]

    def far_xy():
        a, b, c8 = lane // 4 % 4, lane % 4, lane // 16
        gx = (c8 % 4).astype(F32) * SIDE + SIDE * pick(a, OFFSET)
        dx = TB[0] - gx
        for half in range(2):
            gy = (c8 // 4 + 2 * half).astype(F32) * SIDE + SIDE * pick(b, OFFSET)
            dy = TB[1] - gy
            DXY[half] = dx * dx + (dy * dy + SOFTEN)

    def plane_z():
        gz = level_of.astype(F32) * SIDE + SIDE * pick(lane % 4, OFFSET)
        dz = TB[2] - gz
        DXY[0] = dz * dz + SOFTEN
        for b in range(4):
            dy = TB[1] - OFFSET[b]
            DXY[1 + b] = dy * dy

    def far_dz2(lev, d):
        dz = TB[2] - ((g - 1 + lev).astype(F32) * SIDE + SIDE * OFFSET[d])
        return dz * dz

    def plane_xz2(a):
        dx = TB[0] - pick_scalar(a, OFFSET)
        return dx * dx + DXY[0]

    def store_green(block, half, r2):
        for v, values in enumerate(green(r2)):
            G[block, v, half * 128 : half * 128 + 128, :] = values

    def proxy_columns():
        r = iota((128, 128), 0)
        a, b, c8 = r // 4 % 4, r % 4, r // 16
        GC[0] = (c8 % 4).astype(F32) * SIDE + SIDE * pick(a, OFFSET)
        for half in range(2):
            GC[1 + half] = (c8 // 4 + 2 * half).astype(F32) * SIDE + SIDE * pick(b, OFFSET)
        plane = (g + 32 - (r // 8 + 16 * (r // 4 % 2))) % 32
        GC[3] = plane.astype(F32) * SIDE + SIDE * pick(r % 4, OFFSET)

    def dense(lo, hi):
        def cell(t, carry):
            tx, ty, tz = (pts[k, pl.ds(t, 1), :] for k in range(3))
            dx = tx - GC[0]
            dx2 = dx * dx + SOFTEN
            for half in range(2):
                dy = ty - GC[1 + half]
                DS[half] = dx2 + dy * dy
            dz = tz - GC[3]
            DS[2] = dz * dz + SOFTEN

            def far(lev, c):
                for d in range(4):
                    dz = tz - ((g - 1 + lev).astype(F32) * SIDE + SIDE * OFFSET[d])
                    for half in range(2):
                        store_green(t * DENSE + lev * 4 + d, half, DS[half] + dz * dz)
                return c

            lax.fori_loop(0, 3, far, 0, unroll=3)

            def planes(j, c):
                for i in range(2):
                    dx = tx - pick_scalar(2 * j + i, OFFSET)
                    for b in range(4):
                        dy = ty - OFFSET[b]
                        at = t * DENSE + FAR + j * 4 + i * 2 + b // 2
                        store_green(at, b % 2, DS[2] + (dx * dx + dy * dy))
                return c

            lax.fori_loop(0, 2, planes, 0, unroll=2)
            return carry

        lax.fori_loop(lo, hi, cell, 0)

    def near_slot(t, n):
        cell = near[t, n]
        return jnp.where(cell >= 0, jnp.clip(cell - 16 * (g - 1), 0, 47), 48)

    def near_r2(slot):
        lev, c = slot // 16, slot % 16
        total = None
        for k in range(3):
            d = TB[k] - PR[lev, k, pl.ds(c, 1), :]
            total = d * d + SOFTEN if total is None else total + d * d
        return total

    def near_green(cells):
        count = NEAREST[cells[0]]

        def cell(i, carry):
            t = pick_int(i, cells)
            off = pick_int(i, [FIRST[c] for c in cells])
            columns(t)
            for n in range(count):
                for v, values in enumerate(green(near_r2(near_slot(t, n)))):
                    GN[off + n, v] = values
            return carry

        lax.fori_loop(0, len(cells), cell, 0)

    D0[...] = 2.0 * (orb[0] * orb[0] + orb[1] * orb[1])
    PR[1] = pts[...]
    PR[3] = jnp.zeros((3, 16, 128), F32)
    CV[3] = jnp.zeros((16, 128), F32)
    SV[3] = jnp.zeros((2, 16, 128), F32)
    row16 = iota((16, 128), 0)
    ux = (pts[0] - (row16 % 4).astype(F32) * SIDE) * (2.0 / SIDE) - 1.0
    uy = (pts[1] - (row16 // 4).astype(F32) * SIDE) * (2.0 / SIDE) - 1.0
    uz = (pts[2] - g.astype(F32) * SIDE) * (2.0 / SIDE) - 1.0
    for k, u in enumerate((ux, uy, uz)):
        for a, w in enumerate(lagrange(u)):
            LG[k, a] = w
    for k in range(2):
        for a, w in enumerate(lagrange(2.0 * pts[k] - 1.0)):
            LP[k, a] = w
    row8 = iota((8, 128), 0)
    for c in range(16):
        one = slice(c, c + 1)
        ycell = select_rows(row8 % 4, [LG[1, b, one, :] for b in range(4)])
        yplane = select_rows(row8 % 4, [LP[1, b, one, :] for b in range(4)])
        for k in range(2):
            xcell = jnp.where(row8 < 4, LG[0, 2 * k, one, :], LG[0, 2 * k + 1, one, :])
            xplane = jnp.where(row8 < 4, LP[0, 2 * k, one, :], LP[0, 2 * k + 1, one, :])
            at = c % 8 * 16 + k * 8
            A[c // 8, at : at + 8, :] = xcell * ycell
            AP[k * 8 : k * 8 + 8, c * 128 : c * 128 + 128] = xplane * yplane

    def masks(t, carry):
        lev = g - 1 + row8 // 2
        cell = lev * 16 + row8 % 2 * 8 + lane // 16
        hit = (lev < 0) | (lev > 31)
        for n in range(27):
            hit = hit | (cell == near[t, n])
        FM[t] = jnp.where(hit, 0.0, 1.0)
        return carry

    lax.fori_loop(0, 16, masks, 0)
    proxy_columns()
    dense(0, 4)
    pl.semaphore_wait(barrier, len(partners))

    spread = [copy(D0, RA.at[d - 1], 0, other_z(d)) for d in range(1, 16)]
    begin(spread)
    edge_points = rim(PR, 1)
    begin(edge_points)
    dense(4, 12)
    finish(edge_points)
    near_green(CORNERS)
    all_of(RA, 0, other_z(1))
    total = D0[...]
    for d in range(15):
        total = total + RA[d]
    weight = qw[...] * (SIDE**3 / 128)
    CV[1] = weight * total

    def moments(values, cells):
        tiles = []
        for c in range(16):
            one = slice(c, c + 1)
            z = select_rows(row8 % 4, [LG[2, d, one, :] for d in range(4)])
            parts = [v[one, :] for v in values]
            tiles.append(z * jnp.where(row8 < 4, parts[0], parts[1] if len(parts) > 1 else 0.0))
        for half in range(2):
            rows = jnp.concatenate(tiles[half * 8 : half * 8 + 8], axis=0)
            every = lax.dot_general(rows, A[half], LANES, precision=HI, preferred_element_type=F32)
            total = jnp.zeros((8, 128), F32)
            for c in range(8):
                total = jnp.where(lane // 16 == c, every[c * 8 : c * 8 + 8], total)
            cells[1, half] = total
        wide = jnp.concatenate(tiles, axis=1)
        return lax.dot_general(wide, AP[...], LANES, precision=HI, preferred_element_type=F32)

    def send_planes(small, own, got, i):
        own[...] = jnp.zeros((8, 128), F32)
        own[:, 0:16] = small
        got[0] = own[...]
        begin([copy(own, got.at[d], i, other_g(d)) for d in range(1, 32)])

    def take_planes(got, i, count):
        all_of(got.at[1:32], i, other_g(1))
        low = got[0:16].reshape(128, 128).T[0:16]
        high = got[16:32].reshape(128, 128).T[0:16]
        first = lane // 4 % 2 == 0
        parts = [jnp.where(first, low, pltpu.roll(high, 4, 1))]
        if count == 2:
            parts.append(jnp.where(first, pltpu.roll(low, 124, 1), high))
        for v, part in enumerate(parts):
            ZF[v] = jnp.where(jnp.abs(level_of - g) >= 2, part, 0.0)

    edge_charge = rim(CV, 3)
    begin(edge_charge)
    small = moments([CV.at[1]], MC)
    edge_moments = rim(MC, 5)
    begin(edge_moments)
    send_planes(small, QC, RC, 7)
    dense(12, 14)
    near_green(INNER[:1])
    finish(edge_charge)
    finish(edge_moments)

    columns(o)
    acc = jnp.zeros((128, 128), F32)

    def near_hartree(p, acc):
        for i in range(3):
            slot = near_slot(o, 3 * p + i)
            acc = acc + lax.rsqrt(near_r2(slot)) * CV[slot // 16, pl.ds(slot % 16, 1), :]
        return acc

    acc = lax.fori_loop(0, near_count(o) // 3, near_hartree, acc)
    far_xy()

    def far_hartree(lev, acc):
        for half in range(2):
            mask = FM[o, pl.ds(lev * 2 + half, 1), :]
            for d in range(4):
                row = MC[lev, half, d : d + 1, :] * mask
                acc = acc + lax.rsqrt(DXY[half] + far_dz2(lev, d)) * row
        return acc

    acc = lax.fori_loop(0, 3, far_hartree, acc, unroll=3)
    plane_z()
    take_planes(RC, 7, 1)

    def plane_hartree(a, acc):
        xz2 = plane_xz2(a)
        for b in range(4):
            acc = acc + lax.rsqrt(xz2 + DXY[1 + b]) * ZF[0, pl.ds(a * 4 + b, 1), :]
        return acc

    acc = lax.fori_loop(0, 4, plane_hartree, acc, unroll=4)
    HG[0] = jnp.sum(acc.T, axis=0, keepdims=True)
    begin([copy(HG.at[0], HG.at[d], 8, other_z(d)) for d in range(1, 16)])
    near_green(EDGES)
    dense(14, 15)
    all_of(HG.at[1:16], 8, other_z(1))
    for d in range(16):
        hart[pl.ds((o + 16 - d) % 16, 1), :] = HG[d]

    scaled = weight * (ext[...] + hart[...])
    for v in range(2):
        SV[1, v] = scaled * orb[v]
    edge_sources = rim(SV, 9)
    begin(edge_sources)
    small = moments([SV.at[1, 0], SV.at[1, 1]], MS)
    edge_moments = rim(MS, 11)
    begin(edge_moments)
    send_planes(small, QS, RS, 13)
    near_green(INNER[1:])
    dense(15, 16)

    finish(edge_sources)
    finish(edge_moments)
    for v in range(2):
        for lev in range(3):
            for d in range(4):
                r = v * 4 + d
                rows = [MS[lev, half, r : r + 1, :] for half in range(2)]
                VF[lev * 4 + d, v] = hi_lo(jnp.concatenate(rows, axis=1))

    def product(rows, block, v):
        return lax.dot_general(
            rows, G[block, v], (((1,), (0,)), ((), ())), preferred_element_type=F32
        )

    def local(cells):
        def cell(i, carry):
            t = pick_int(i, cells)
            off = pick_int(i, [FIRST[c] for c in cells])
            far = [jnp.zeros((16, 128), F32) for _ in range(2)]
            for lev in range(3):
                mask = jnp.concatenate(
                    [
                        jnp.broadcast_to(FM[t, lev * 2 + half : lev * 2 + half + 1, :], (16, 128))
                        for half in range(2)
                    ],
                    axis=1,
                ).astype(BF16)
                for d in range(4):
                    k = lev * 4 + d
                    for v in range(2):
                        far[v] = far[v] + product(VF[k, v] * mask, t * DENSE + k, v)
            slots = [near_slot(t, n) for n in range(NEAREST[cells[0]])]
            for v in range(2):
                total = None
                for n, slot in enumerate(slots):
                    row = SV[slot // 16, v, pl.ds(slot % 16, 1), :]
                    term = GN[off + n, v].astype(F32) * row
                    total = term if total is None else total + term
                near_row = jnp.sum(total.T, axis=0, keepdims=True)
                FR[v, pl.ds(t, 1), :] = near_row + (far[v][0:1] + far[v][1:2])
            return carry

        lax.fori_loop(0, len(cells), cell, 0, unroll=2)

    local(CORNERS)
    local(EDGES)
    local(INNER)
    take_planes(RS, 13, 2)
    for v in range(2):
        for k in range(PLANE):
            rows = [ZF[v, 2 * k + half : 2 * k + half + 1, :] for half in range(2)]
            VP[k, v] = hi_lo(jnp.concatenate(rows, axis=1))

    def update(t, carry):
        for v in range(2):
            acc = jnp.zeros((16, 128), F32)
            for k in range(PLANE):
                acc = acc + product(VP[k, v], t * DENSE + FAR + k, v)
            row = FR[v, pl.ds(t, 1), :] + (acc[0:1] + acc[1:2])
            out[v, pl.ds(t, 1), :] = SCALE * row
        return carry

    lax.fori_loop(0, 16, update, 0, unroll=2)


def body(orbitals, points, quad_weight, external, screening, level_index, near_cells, far_cells):
    vmem = pl.BlockSpec(memory_space=pltpu.VMEM)
    smem = pl.BlockSpec(memory_space=pltpu.SMEM)

    def f32(*shape):
        return pltpu.VMEM(shape, F32)

    def bf16(*shape):
        return pltpu.VMEM(shape, BF16)

    return pl.pallas_call(
        kernel,
        out_shape=(
            jax.ShapeDtypeStruct((2, 16, 128), F32),
            jax.ShapeDtypeStruct((16, 128), F32),
        ),
        in_specs=[vmem] * 4 + [smem] * 3,
        out_specs=(vmem, vmem),
        scratch_shapes=[
            bf16(16 * DENSE, 2, 256, 128),
            bf16(NEAR, 2, 128, 128),
            f32(3, 128, 128),
            f32(5, 128, 128),
            f32(4, 128, 128),
            f32(3, 128, 128),
            f32(2, 16, 128),
            bf16(FAR, 2, 16, 256),
            bf16(PLANE, 2, 16, 256),
            f32(4, 3, 16, 128),
            f32(4, 16, 128),
            f32(4, 2, 16, 128),
            f32(3, 2, 8, 128),
            f32(3, 2, 8, 128),
            f32(3, 4, 16, 128),
            f32(2, 4, 16, 128),
            f32(2, 128, 128),
            f32(16, 2048),
            f32(16, 128),
            f32(15, 16, 128),
            f32(8, 128),
            f32(32, 8, 128),
            f32(8, 128),
            f32(32, 8, 128),
            f32(2, 16, 128),
            f32(16, 1, 128),
            f32(16, 8, 128),
            pltpu.SemaphoreType.DMA((14,)),
            pltpu.SemaphoreType.DMA((14,)),
        ],
        compiler_params=pltpu.CompilerParams(
            collective_id=0, has_side_effects=True, vmem_limit_bytes=67043328
        ),
        name="green_step",
    )(orbitals, points, quad_weight, external, screening, level_index, near_cells)


def solution(mesh):
    in_specs = (
        P("orb", "space", None),
        P(None, "space", None),
        P("space", None),
        P("space", None),
        P(),
        P("orb"),
        P("space", None),
        P("space", None),
    )
    out_specs = (P("orb", "space", None), P("space", None))
    return jax.shard_map(body, mesh=mesh, in_specs=in_specs, out_specs=out_specs, check_vma=False)
```
